128 devices in a mesh: slab: 16 (over x_hi, z, core), col: 8 (over x_lo, y).
Axes of the slice: x: 4 (x_hi: 2, x_lo: 2; x = x_hi * 2 + x_lo), y: 4, z: 4, core: 2. Of those that a mesh axis runs over, the one named last changes fastest.
Arguments:
- sensitivity: bfloat16 [3, 512, 65536], P(None, 'col', 'slab'), may hold values from -0.03125 to 0.03125
- residual_force: bfloat16 [3, 65536], P(None, 'slab'), may hold values from -6 to 6
- moments: float32 [6, 64, 1024], P(None, 'slab'), as said below
- zone_label: int32 [64, 1024], P('slab'), may hold values from 0 to 511, as said below
- misfit: float32 [64, 1024], P('slab'), may hold values from 0.1 to 10
Outputs:
- hessian: float32 [512, 512], P('col', 'slab')
- gradient: float32 [512], replicated
- zone_misfit: float32 [512], replicated
The draws below stay inside these ranges and needn't reach their ends.
Inputs may be any that keep to these rules, and one draw needn't show every extreme that they name: zone_label is the box of a 8 x 8 x 8 partition of the specimen that holds the element, the in-plane box borders displaced by at most one element; every zone occurs. `moments`: each element's moment matrix is symmetric with positive diagonal, and each diagonal entry exceeds the sum of the magnitudes of the others in its row.
All inputs are finite; a program needn't handle non-finite values.
Results may differ from the reference program's by a relative error of at most 0.0003.
Values may be sent and summed in bfloat16 or wider, within the bound.
A program may use at most 128 MiB of HBM per device.

```python
import math
import jax
import jax.numpy as jnp
from jax import lax

GX = 64
GY = 16
ZB = 8
P_SIZE = 512
NLAYERS = 64
NODES = 65536


def draw_moments(key, part):
    count = NLAYERS * GX * GY
    keys = jax.random.split(key, 2)
    diag = jnp.exp(jax.random.uniform(keys[0], (3, count), jnp.float32, math.log(0.5), math.log(2.0)))
    coupling = jax.random.uniform(keys[1], (3, count), jnp.float32, -0.45, 0.45)
    off_xy = coupling[0] * jnp.minimum(diag[0], diag[1])
    off_xz = coupling[1] * jnp.minimum(diag[0], diag[2])
    off_yz = coupling[2] * jnp.minimum(diag[1], diag[2])
    whole = jnp.concatenate([diag, jnp.stack([off_xy, off_xz, off_yz])], axis=0)
    return whole.reshape(6, NLAYERS, GX * GY)


def draw_zone_label(key, part):
    keys = jax.random.split(key, 2)
    layer = jnp.arange(NLAYERS, dtype=jnp.int32)[:, None]
    cell = jnp.arange(GX * GY, dtype=jnp.int32)[None, :]
    pos_x = cell // GY
    pos_y = cell % GY
    wide_x = GX // ZB
    wide_y = GY // ZB
    shape = (NLAYERS, GX * GY)
    jitter_x = jax.random.randint(keys[0], shape, -1, 2, jnp.int32) * (pos_x % wide_x != 0).astype(jnp.int32)
    jitter_y = jax.random.randint(keys[1], shape, -1, 2, jnp.int32) * (pos_y % wide_y != 0).astype(jnp.int32)
    box_x = jnp.clip(pos_x + jitter_x, 0, GX - 1) // wide_x
    box_y = jnp.clip(pos_y + jitter_y, 0, GY - 1) // wide_y
    box_z = layer // (NLAYERS // ZB) + jnp.zeros(shape, jnp.int32)
    return ((box_z * ZB + box_x) * ZB + box_y).astype(jnp.int32)


def block_levels(rng, dims, cuts, least, top_value):
    level, own = 1.0, jax.random.fold_in(rng, 6)
    for position, shards_of in cuts:
        heights = jnp.exp(jax.random.uniform(jax.random.fold_in(own, position), (shards_of,), jnp.float32, least / len(cuts), top_value / len(cuts)))
        level = level * jnp.repeat(heights, dims[position] // shards_of).reshape([-1 if axis == position else 1 for axis in range(len(dims))])
    return level


def bell_draw(key, dims, scale, bound, shards=(), kind=jnp.bfloat16):
    result = jax.random.normal(key, dims, jnp.float32) * scale
    if len(shards) > 0:
        result = block_levels(key, dims, shards, -0.22, 0.18) * result
    return jnp.clip(result, min=-bound, max=bound).astype(kind)


def setup_inputs(seed: int = 0) -> dict:
    arg_keys = jax.random.split(jax.random.key(seed), 6)
    sensitivity = bell_draw(arg_keys[0], (3, P_SIZE, NODES), ((3 * NODES) ** -0.5), 0.03125, ((1, 8), (2, 16)))
    residual_force = bell_draw(arg_keys[1], (3, NODES), 1.0, 6.0, ((1, 16),))
    moments = draw_moments(jax.random.fold_in(arg_keys[5], 71), 0)
    zone_label = draw_zone_label(jax.random.fold_in(arg_keys[5], 71), 0)
    misfit = jnp.clip(jnp.exp(math.log(10.0) - 4.6051702 * jax.random.uniform(arg_keys[4], (NLAYERS, GX * GY), jnp.float32) ** block_levels(arg_keys[4], (NLAYERS, GX * GY), ((0, 16),), -0.2, 0.2)), 0.1, 10.0)
    return {"sensitivity": sensitivity, "residual_force": residual_force, "moments": moments, "zone_label": zone_label, "misfit": misfit}


third = 1.0 / 3.0
sixth = 1.0 / 6.0


def mix_pair(first, second):
    return third * first + sixth * second, sixth * first + third * second


def shift_ahead(field, step, keep):
    moved = jnp.concatenate([field[..., step:], jnp.zeros_like(field[..., :step])], axis=-1)
    if keep is None:
        return moved
    return jnp.where(keep, moved, 0.0)


def shift_behind(field, step, keep):
    moved = jnp.concatenate([jnp.zeros_like(field[..., :step]), field[..., :-step]], axis=-1)
    if keep is None:
        return moved
    return jnp.where(keep, moved, 0.0)


def apply_moments(moments, field):
    comps = [moments[k][None, :] for k in range(6)]
    first, second, last = field[0], field[1], field[2]
    out_x = comps[0] * first + comps[3] * second + comps[4] * last
    out_y = comps[3] * first + comps[1] * second + comps[5] * last
    out_z = comps[4] * first + comps[5] * second + comps[2] * last
    return jnp.stack([out_x, out_y, out_z])


def element_layer(lower, upper, moments):
    plane = lower.shape[-1]
    pos_y = jnp.arange(plane, dtype=jnp.int32) % GY
    not_last = pos_y != GY - 1
    not_first = pos_y != 0
    mixed_z = mix_pair(lower, upper)
    results = []
    for side_z in range(2):
        field = mixed_z[side_z]
        mixed_x = mix_pair(field, shift_ahead(field, GY, None))
        values = []
        for side_x in range(2):
            layer = mixed_x[side_x]
            mixed_y = mix_pair(layer, shift_ahead(layer, 1, not_last))
            values.append([apply_moments(moments, mixed_y[side_y]) for side_y in range(2)])
        total = values[0][0]
        total = total + shift_behind(values[1][0], GY, None)
        total = total + shift_behind(values[0][1], 1, not_first)
        total = total + shift_behind(shift_behind(values[1][1], 1, not_first), GY, None)
        results.append(total)
    return results[0], results[1]


def reference(sensitivity, residual_force, moments, zone_label, misfit):
    cols = sensitivity.shape[1]
    layers = moments.shape[1]
    plane = GX * GY
    field = sensitivity.reshape(3, cols, layers, plane)

    def one_layer(level):
        lower = lax.dynamic_index_in_dim(field, level, 2, keepdims=False).astype(jnp.float32)
        above_index = jnp.minimum(level + 1, layers - 1).astype(jnp.int32)
        upper = lax.dynamic_index_in_dim(field, above_index, 2, keepdims=False).astype(jnp.float32)
        upper = jnp.where(level + 1 < layers, upper, jnp.zeros_like(upper))
        layer_moments = lax.dynamic_index_in_dim(moments, level, 1, keepdims=False)
        return element_layer(lower, upper, layer_moments)

    to_lower, to_upper = lax.map(one_layer, jnp.arange(layers, dtype=jnp.int32))
    from_below = jnp.concatenate([jnp.zeros_like(to_upper[:1]), to_upper[:-1]], axis=0)
    stacked = (from_below + to_lower).astype(jnp.bfloat16)
    image = jnp.moveaxis(stacked, 0, 2).reshape(3, cols, layers * plane)
    hessian = lax.dot_general(image, sensitivity, (((0, 2), (0, 2)), ((), ())), preferred_element_type=jnp.float32)
    gradient = lax.dot_general(residual_force, sensitivity, (((0, 1), (0, 2)), ((), ())), preferred_element_type=jnp.float32)
    total = zone_label.size
    sums = jax.ops.segment_sum(misfit.reshape(-1), zone_label.reshape(-1), num_segments=cols)
    zone_misfit = sums * (cols / total)
    return hessian, gradient, zone_misfit
```

```python
import functools

import jax
import jax.numpy as jnp
from jax import lax
from jax.experimental import pallas as pl
from jax.experimental.pallas import tpu as pltpu
from jax.sharding import PartitionSpec as P

MESH = pl.DeviceIdType.MESH
GX = 64
GY = 16
PLANE = GX * GY
LAYERS = 4
COLS = 64
WIDTH = 512
TILE = 128
KW = 768
ROWS = WIDTH + 16
BF = jnp.bfloat16
F32 = jnp.float32
NT = (((1,), (1,)), ((), ()))
OFFS = ((0, 1), (0, 3), (1, 0), (0, 2), (1, 1), (1, 3), (1, 2))


def iota(shape, dim):
    return lax.broadcasted_iota(jnp.int32, shape, dim)


def mix_weights():
    src = jnp.arange(2 * TILE, dtype=jnp.int32)[None, :, None]
    elem = jnp.arange(TILE, dtype=jnp.int32)[None, None, :]
    layer = jnp.arange(LAYERS + 1, dtype=jnp.int32)[:, None, None]
    ex, ey = elem // GY, elem % GY
    parts = []
    for b in range(2):
        for c in range(2):
            total = jnp.zeros((LAYERS + 1, 2 * TILE, TILE), F32)
            for b2 in range(2):
                for c2 in range(2):
                    weight = (2.0 if b == b2 else 1.0) * (2.0 if c == c2 else 1.0)
                    nx, ny = ex + b2, ey + c2
                    node = jnp.where(nx < 8, nx * GY + ny, TILE + layer * GY + ny)
                    total = total + jnp.where((src == node) & (ny < GY), weight, 0.0)
            parts.append(total)
    return jnp.concatenate(parts, axis=2).astype(BF)


def pick_weights():
    src = jnp.arange((LAYERS + 1) * TILE, dtype=jnp.int32)[:, None]
    dst = jnp.arange(TILE, dtype=jnp.int32)[None, :]
    return ((src // TILE == dst // GY) & (src % TILE == dst % GY)).astype(BF)


def kernel(
    s_any, res_ref, mom_ref, lab_ref, mis_ref, w_ref, pick_ref,
    h_out, e_out,
    sloc, zbuf, hal, sbuf, img, fbuf, gbuf, hacc, hrecv, erecv, hs, r1, m2, r2,
    loc_sem, z_sem, ss, rs, own_sem, p0_sem, s1, q1, s2, q2,
):
    s = lax.axis_index("slab")
    c = lax.axis_index("col")
    core = lax.rem(s, 2)
    z = lax.rem(s // 2, 4)
    xh = s // 8
    xl = c // 4
    y = lax.rem(c, 4)
    d = s // 2

    def col_peer(dx, dy):
        return lax.rem(xl + dx, 2) * 4 + lax.rem(y + dy + 4, 4)

    def slab_peer(dx, dz):
        return (lax.rem(xh + dx, 2) * 4 + lax.rem(z + dz + 4, 4)) * 2 + core

    partner = s + 1 - 2 * core
    bar = pltpu.get_barrier_semaphore()
    for dx, dy in OFFS:
        pl.semaphore_signal(bar, inc=1, device_id=(s, col_peer(dx, dy)), device_id_type=MESH)
        pl.semaphore_signal(bar, inc=1, device_id=(slab_peer(dx, dy), c), device_id_type=MESH)
    pl.semaphore_signal(bar, inc=1, device_id=(partner, c), device_id_type=MESH)
    pl.semaphore_signal(bar, inc=1, device_id=(lax.rem(s + 1, 16), c), device_id_type=MESH)
    pl.semaphore_signal(bar, inc=1, device_id=(lax.rem(s + 15, 16), c), device_id_type=MESH)
    load = pltpu.make_async_copy(s_any, sloc, loc_sem)
    load.start()

    def tile_at(ref, who, t):
        return ref.at[:, pl.ds(pl.multiple_of(who * COLS, COLS), COLS), pl.ds(t * TILE, TILE)]

    def lanes(l, who):
        return pl.ds(pl.multiple_of(l * PLANE + who * TILE, TILE), TILE)

    for l in range(LAYERS):
        pltpu.make_async_copy(s_any.at[:, :, lanes(l, c)], tile_at(sbuf, c, l), rs.at[c, l]).start()

    @pl.when(s == 15)
    def _():
        zbuf[...] = jnp.zeros_like(zbuf)

    pl.semaphore_wait(bar, 17)
    down = pltpu.make_async_remote_copy(
        src_ref=s_any.at[:, :, pl.ds(0, PLANE)], dst_ref=zbuf, send_sem=z_sem.at[0], recv_sem=z_sem.at[1],
        device_id=(lax.rem(s + 15, 16), c), device_id_type=MESH)

    @pl.when(s > 0)
    def _():
        down.start()

    def send(i, t):
        dx, dy = OFFS[i]
        who = col_peer(dx, dy)
        if t < LAYERS:
            src = s_any.at[:, :, lanes(t, who)]
        elif t == LAYERS:
            src = zbuf.at[:, :, lanes(0, who)]
        else:
            src = hal.at[who]
        return pltpu.make_async_remote_copy(
            src_ref=src, dst_ref=tile_at(sbuf, c, t), send_sem=ss.at[i, t], recv_sem=rs.at[c, t],
            device_id=(s, who), device_id_type=MESH)

    early = 3
    for i in range(early):
        for t in range(LAYERS):
            send(i, t).start()

    ctile = pl.ds(pl.multiple_of(c * TILE, TILE), TILE)
    for k in range(6):
        for l in range(LAYERS):
            gbuf[k, l] = jnp.broadcast_to(mom_ref[k, pl.ds(l, 1), ctile] * (1.0 / 216.0), (16, TILE))
    row16 = iota((16, TILE), 0)
    for k in range(3):
        for t in range(LAYERS + 2):
            if t < LAYERS:
                row = jnp.broadcast_to(res_ref[pl.ds(k, 1), lanes(t, c)].astype(F32), (16, TILE))
                val = jnp.where(row16 == 0, row, 0.0)
            else:
                val = jnp.zeros((16, TILE), F32)
            img[k, WIDTH:ROWS, t * TILE:(t + 1) * TILE] = val.astype(BF)
    parts = []
    for l in range(LAYERS):
        x = mis_ref[pl.ds(l, 1), ctile]
        hi = x.astype(BF).astype(F32)
        mid = (x - hi).astype(BF).astype(F32)
        lo = x - hi - mid
        full = jnp.where(row16 == 1, jnp.broadcast_to(hi, (16, TILE)), 0.0)
        full = jnp.where(row16 == 2, jnp.broadcast_to(mid, (16, TILE)), full)
        full = jnp.where(row16 == 3, jnp.broadcast_to(lo, (16, TILE)), full)
        parts.append(full.astype(BF))
    zone_lhs = jnp.concatenate(parts, axis=1)
    for half in range(2):
        row = iota((256, TILE), 0)
        zone_id = (row // 32) * 64 + half * 32 + lax.rem(row, 32)
        hot = jnp.concatenate([
            jnp.where(jnp.broadcast_to(lab_ref[pl.ds(l, 1), ctile], (256, TILE)) == zone_id, 1.0, 0.0).astype(BF)
            for l in range(LAYERS)], axis=1)
        hacc[half, WIDTH:ROWS, :] = lax.dot_general(zone_lhs, hot, NT, preferred_element_type=F32)

    load.wait()

    @pl.when(s < 15)
    def _():
        down.wait_recv()

    for who in range(8):
        if who == 7:
            hal[7] = jnp.zeros((3, COLS, TILE), BF)
        else:
            at = (who + 1) * TILE
            tiles = [sloc[:, :, l * PLANE + at:l * PLANE + at + TILE].reshape(3 * COLS, TILE) for l in range(LAYERS)]
            tiles.append(zbuf[:, :, at:at + TILE].reshape(3 * COLS, TILE))
            got = jnp.dot(jnp.concatenate(tiles, axis=1), pick_ref[...], preferred_element_type=F32)
            hal[who] = got.astype(BF).reshape(3, COLS, TILE)

    for i in range(early):
        for t in (LAYERS, LAYERS + 1):
            send(i, t).start()
    for i in range(early, 7):
        for t in range(LAYERS + 2):
            send(i, t).start()
    pltpu.make_async_copy(zbuf.at[:, :, lanes(0, c)], tile_at(sbuf, c, LAYERS), rs.at[c, LAYERS]).start()
    pltpu.make_async_copy(hal.at[c], tile_at(sbuf, c, LAYERS + 1), rs.at[c, LAYERS + 1]).start()

    lane = iota((16, TILE), 1)
    not_first = lax.rem(lane, GY) != 0
    inside = lane >= GY

    def block(src):
        for t in range(LAYERS + 2):
            at = tile_at(sbuf, src, t)
            pltpu.make_async_copy(at, at, rs.at[src, t]).wait()
        base = pl.multiple_of(src * COLS, COLS)
        halo = sbuf[:, pl.ds(base, COLS), KW - TILE:KW].reshape(3 * COLS, TILE)
        for l in range(LAYERS + 1):
            here = sbuf[:, pl.ds(base, COLS), l * TILE:(l + 1) * TILE].reshape(3 * COLS, TILE)
            both = jnp.concatenate([here, halo], axis=1)
            got = jnp.dot(both, w_ref[l], preferred_element_type=F32)
            fbuf[l] = got.reshape(3, COLS, 4 * TILE)

        @pl.loop(0, COLS // 16)
        def _(r):
            rows = pl.ds(pl.multiple_of(r * 16, 16), 16)
            dest = pl.ds(pl.multiple_of(base + r * 16, 16), 16)
            carry = [[None] * 3 for _ in range(4)]
            edge = [jnp.zeros((16, TILE), F32) for _ in range(3)]
            for n in range(LAYERS + 1):
                unit = [[None] * 3 for _ in range(4)]
                if n < LAYERS:
                    g = [gbuf[k, n] for k in range(6)]
                    for q in range(4):
                        low, high = [], []
                        for k in range(3):
                            first = fbuf[n, k, rows, q * TILE:(q + 1) * TILE]
                            second = fbuf[n + 1, k, rows, q * TILE:(q + 1) * TILE]
                            both = first + second
                            low.append(first + both)
                            high.append(second + both)

                        def apply(v):
                            return [
                                g[0] * v[0] + g[3] * v[1] + g[4] * v[2],
                                g[3] * v[0] + g[1] * v[1] + g[5] * v[2],
                                g[4] * v[0] + g[5] * v[1] + g[2] * v[2],
                            ]

                        low, high = apply(low), apply(high)
                        for k in range(3):
                            unit[q][k] = low[k] if n == 0 else carry[q][k] + low[k]
                            carry[q][k] = high[k]
                else:
                    unit = carry
                for k in range(3):
                    near = unit[0][k] + jnp.where(not_first, pltpu.roll(unit[1][k], 1, 1), 0.0)
                    far = unit[2][k] + jnp.where(not_first, pltpu.roll(unit[3][k], 1, 1), 0.0)
                    moved = pltpu.roll(far, GY, 1)
                    img[k, dest, n * TILE:(n + 1) * TILE] = (near + jnp.where(inside, moved, 0.0)).astype(BF)
                    if n > 0:
                        moved = pltpu.roll(far, GY * (n + 1), 1)
                    edge[k] = jnp.where((lane >= GY * n) & (lane < GY * (n + 1)), moved, edge[k])
            for k in range(3):
                img[k, dest, KW - TILE:KW] = edge[k].astype(BF)

    block(c)
    for dx, dy in OFFS:
        block(col_peer(dx, -dy))

    def panel(half):
        total = None
        for k in range(3):
            rhs = jnp.concatenate(
                [sbuf[k, pl.ds(pl.multiple_of(e * 64 + half * 32, 32), 32), :] for e in range(8)], axis=0)
            got = lax.dot_general(img[k], rhs, NT, preferred_element_type=F32)
            total = got if total is None else total + got
        hacc[half, 0:WIDTH, :] = total[:WIDTH]
        hacc[half, WIDTH:ROWS, :] = hacc[half, WIDTH:ROWS, :] + total[WIDTH:]

    other = 1 - core
    panel(other)
    swap = pltpu.make_async_remote_copy(
        src_ref=hacc.at[other], dst_ref=hrecv, send_sem=p0_sem.at[0], recv_sem=p0_sem.at[1],
        device_id=(partner, c), device_id_type=MESH)
    swap.start()
    panel(core)
    swap_e = pltpu.make_async_remote_copy(
        src_ref=hacc.at[core, pl.ds(WIDTH, 16), :], dst_ref=erecv, send_sem=p0_sem.at[2], recv_sem=p0_sem.at[3],
        device_id=(partner, c), device_id_type=MESH)
    swap_e.start()
    swap.wait_recv()
    swap_e.wait_recv()
    mine = hacc[core, WIDTH:WIDTH + 8, :] + hrecv[WIDTH:WIDTH + 8, :]
    theirs = hacc[other, WIDTH:WIDTH + 8, :] + erecv[0:8, :]
    even = jnp.where(core == 0, mine, theirs)
    odd = jnp.where(core == 0, theirs, mine)
    for who in range(8):
        hs[who, 0:COLS, :] = hacc[core, who * COLS:(who + 1) * COLS, :] + hrecv[who * COLS:(who + 1) * COLS, :]
        hs[who, COLS:COLS + 8, :] = even
        hs[who, COLS + 8:COLS + 16, :] = odd

    def send1(i):
        who = col_peer(*OFFS[i])
        return pltpu.make_async_remote_copy(
            src_ref=hs.at[who], dst_ref=r1.at[c], send_sem=s1.at[i], recv_sem=q1.at[c],
            device_id=(s, who), device_id_type=MESH)

    for i in range(7):
        send1(i).start()
    r1[c] = hs[c]
    for dx, dy in OFFS:
        who = col_peer(dx, -dy)
        pltpu.make_async_copy(r1.at[who], r1.at[who], q1.at[who]).wait()
    total = r1[0]
    for who in range(1, 8):
        total = total + r1[who]
    tail = total[COLS:COLS + 16]
    tail_rows = []
    for j in range(2):
        for half in range(2):
            for a in range(2):
                piece = tail[half * 8:half * 8 + 8, a * TILE:(a + 1) * TILE]
                if j == 0:
                    tail_rows.append(piece[0:1])
                else:
                    tail_rows.append(piece[1:2] + piece[2:3] + piece[3:4])
    ext = jnp.concatenate(tail_rows, axis=0)
    group = lane // 32
    for e in range(8):
        a, b = e // 4, e % 4
        packed = None
        for g in range(4):
            piece = total[16 * g:16 * g + 16, a * TILE:(a + 1) * TILE]
            shift = (32 * g - 32 * b) % TILE
            if shift:
                piece = pltpu.roll(piece, shift, 1)
            packed = piece if packed is None else jnp.where(group == g, piece, packed)
        m2[e, 0:16, :] = packed
        m2[e, 16:24, :] = ext

    def send2(i):
        to = slab_peer(*OFFS[i])
        return pltpu.make_async_remote_copy(
            src_ref=m2.at[to // 2], dst_ref=r2.at[d], send_sem=s2.at[i], recv_sem=q2.at[d],
            device_id=(to, c), device_id_type=MESH)

    for i in range(7):
        send2(i).start()
    r2[d] = m2[d]
    for dx, dz in OFFS:
        who = slab_peer(dx, -dz) // 2
        pltpu.make_async_copy(r2.at[who], r2.at[who], q2.at[who]).wait()
    total = r2[0]
    for who in range(1, 8):
        total = total + r2[who]
    for g in range(4):
        piece = total[0:16]
        if g:
            piece = pltpu.roll(piece, TILE - 32 * g, 1)
        h_out[16 * g:16 * g + 16, :] = piece[:, 0:32]
    ext = total[16:24]
    lane1 = iota((1, TILE), 1) // 32
    for j in range(2):
        for t in range(4):
            full = None
            for p in range(4):
                e, half = 2 * t + p // 2, p % 2
                row = j * 4 + half * 2 + e // 4
                piece = ext[row:row + 1]
                shift = (32 * p - 32 * (e % 4)) % TILE
                if shift:
                    piece = pltpu.roll(piece, shift, 1)
                full = piece if full is None else jnp.where(lane1 == p, piece, full)
            if j == 1:
                full = full * (WIDTH / 65536)
            e_out[4 * j + t:4 * j + t + 1, :] = full

    @pl.when(s > 0)
    def _():
        down.wait_send()

    for i in range(7):
        for t in range(LAYERS + 2):
            send(i, t).wait_send()
        send1(i).wait_send()
        send2(i).wait_send()
    swap.wait_send()
    swap_e.wait_send()


def on_device(sensitivity, residual_force, moments, zone_label, misfit):
    any_spec = pl.BlockSpec(memory_space=pl.ANY)
    vmem = pl.BlockSpec(memory_space=pltpu.VMEM)
    dma = pltpu.SemaphoreType.DMA
    h, e = pl.pallas_call(
        kernel,
        name="gauss_newton",
        out_shape=(jax.ShapeDtypeStruct((COLS, 32), F32), jax.ShapeDtypeStruct((8, TILE), F32)),
        in_specs=[any_spec] + [vmem] * 6,
        out_specs=(vmem, vmem),
        scratch_shapes=[
            pltpu.VMEM((3, COLS, LAYERS * PLANE), BF),
            pltpu.VMEM((3, COLS, PLANE), BF),
            pltpu.VMEM((8, 3, COLS, TILE), BF),
            pltpu.VMEM((3, WIDTH, KW), BF),
            pltpu.VMEM((3, ROWS, KW), BF),
            pltpu.VMEM((LAYERS + 1, 3, COLS, 4 * TILE), F32),
            pltpu.VMEM((6, LAYERS, 16, TILE), F32),
            pltpu.VMEM((2, ROWS, 256), F32),
            pltpu.VMEM((ROWS, 256), F32),
            pltpu.VMEM((16, 256), F32),
            pltpu.VMEM((8, COLS + 16, 256), F32),
            pltpu.VMEM((8, COLS + 16, 256), F32),
            pltpu.VMEM((8, 24, TILE), F32),
            pltpu.VMEM((8, 24, TILE), F32),
            dma(()), dma((2,)), dma((7, 6)), dma((8, 6)), dma(()), dma((4,)),
            dma((7,)), dma((8,)), dma((7,)), dma((8,)),
        ],
        compiler_params=pltpu.CompilerParams(collective_id=0, has_side_effects=True, vmem_limit_bytes=48 * 2**20),
    )(sensitivity, residual_force, moments, zone_label, misfit, mix_weights(), pick_weights())
    return h, e[0:4].reshape(WIDTH), e[4:8].reshape(WIDTH)


def solution(mesh):
    in_specs = (
        P(None, "col", "slab"),
        P(None, "slab"),
        P(None, "slab", None),
        P("slab", None),
        P("slab", None),
    )
    out_specs = (P("col", "slab"), P(), P())
    return jax.shard_map(
        on_device, mesh=mesh, in_specs=in_specs, out_specs=out_specs, check_vma=False
    )
```

```python
import jax
import jax.numpy as jnp
from jax import lax
from jax.experimental import pallas as pl
from jax.experimental.pallas import tpu as pltpu
from jax.sharding import PartitionSpec as P

MESH = pl.DeviceIdType.MESH
GX = 64
GY = 16
PLANE = GX * GY
LAYERS = 4
COLS = 64
WIDTH = 512
TILE = 128
KW = 768
EDGE = 3 * 32
PART = 3 * COLS
CHUNK = EDGE + LAYERS * PART
BF = jnp.bfloat16
F32 = jnp.float32
NT = (((1,), (1,)), ((), ()))
OFFS = ((0, 1), (0, 3), (1, 0), (0, 2), (1, 1), (1, 3), (1, 2))


def iota(shape, dim):
    return lax.broadcasted_iota(jnp.int32, shape, dim)


def pair_weight(shift, side):
    return jnp.where(shift == side, 2.0, jnp.where(shift == 1 - side, 1.0, 0.0))


def fill_weights(w_ref, pick_ref):
    src, elem = iota((TILE, TILE), 0), iota((TILE, TILE), 1)
    ex, ey = elem // GY, lax.rem(elem, GY)
    sx, sy = src // GY, lax.rem(src, GY)
    for b in range(2):
        for c in range(2):
            wy = pair_weight(sy - ey, c)
            at = (2 * b + c) * TILE
            near = (pair_weight(sx - ex, b) * wy).astype(BF)
            far = pair_weight(8 - ex, b) * wy
            for l in range(LAYERS + 1):
                w_ref[l, 0:TILE, at:at + TILE] = near
                w_ref[l, TILE:2 * TILE, at:at + TILE] = jnp.where(sx == l, far, 0.0).astype(BF)
    for h in range(2):
        for l in range(LAYERS):
            hit = (src == elem - 64 * h - GY * l) & (src < GY)
            at = (h * LAYERS + l) * TILE
            pick_ref[at:at + TILE, :] = jnp.where(hit, 1.0, 0.0).astype(BF)


def kernel(
    s_any, res_any, mom_any, lab_any, mis_any,
    h_out, g_out, z_out,
    w_ref, pick_ref, res_ref, mom_ref, lab_ref, mis_ref,
    stage, chunk, above, edges, img, fbuf, gbuf, hacc, hrecv, pack, parts,
    esrc, e0, e1, e2,
    in_sem, st_sem, ss, rs, fs, fz, p0_sem, es, er, msem, rsem,
):
    s = lax.axis_index("slab")
    c = lax.axis_index("col")
    core = lax.rem(s, 2)
    z = lax.rem(s // 2, 4)
    xh = s // 8
    xl = c // 4
    y = lax.rem(c, 4)
    d = s // 2

    def col_peer(dx, dy):
        return lax.rem(xl + dx, 2) * 4 + lax.rem(y + dy + 4, 4)

    def slab_peer(dx, dz):
        return (lax.rem(xh + dx, 2) * 4 + lax.rem(z + dz + 4, 4)) * 2 + core

    order = [c] + [col_peer(dx, -dy) for dx, dy in OFFS]
    partner = s + 1 - 2 * core
    below = lax.rem(s + 15, 16)
    bar = pltpu.get_barrier_semaphore()
    for k in range(1, 64):
        to_c = lax.rem(c + k // 8, 8)
        to_d = lax.rem(d + k, 8)
        pl.semaphore_signal(bar, inc=1, device_id=(to_d * 2 + core, to_c), device_id_type=MESH)
    for to in (partner, lax.rem(s + 1, 16), below):
        pl.semaphore_signal(bar, inc=1, device_id=(to, c), device_id_type=MESH)

    def lanes(l, who):
        return pl.ds(pl.multiple_of(l * PLANE + who * TILE, TILE), TILE)

    for who in range(8):
        for l in range(LAYERS):
            for k in range(3):
                at = EDGE + l * PART + k * COLS
                pltpu.make_async_copy(
                    s_any.at[k, :, lanes(l, who)], stage.at[who, pl.ds(at, COLS), :], st_sem.at[who]).start()
    loads = [
        pltpu.make_async_copy(a, b, in_sem.at[i])
        for i, (a, b) in enumerate(((res_any, res_ref), (mom_any, mom_ref), (lab_any, lab_ref), (mis_any, mis_ref)))]
    for load in loads:
        load.start()

    @pl.when(s == 15)
    def _():
        above[...] = jnp.zeros_like(above)

    fill_weights(w_ref, pick_ref)
    for who in range(8):
        at = stage.at[who, pl.ds(EDGE, LAYERS * PART), :]
        pltpu.make_async_copy(at, at, st_sem.at[who]).wait()

    for who in range(8):
        if who == 7:
            stage[7, 0:EDGE, :] = jnp.zeros((EDGE, TILE), BF)
        else:
            tiles = [
                jnp.concatenate([
                    stage[who + 1, EDGE + l * PART + k * COLS + 32 * h:EDGE + l * PART + k * COLS + 32 * h + 32, :]
                    for k in range(3)], axis=0)
                for h in range(2) for l in range(LAYERS)]
            got = jnp.dot(jnp.concatenate(tiles, axis=1), pick_ref[...], preferred_element_type=F32)
            stage[who, 0:EDGE, :] = got.astype(BF)
    pltpu.make_async_copy(stage.at[c], chunk.at[c], rs.at[c]).start()

    pl.semaphore_wait(bar, 66)

    def send(i):
        who = col_peer(*OFFS[i])
        return pltpu.make_async_remote_copy(
            src_ref=stage.at[who], dst_ref=chunk.at[c], send_sem=ss.at[i], recv_sem=rs.at[c],
            device_id=(s, who), device_id_type=MESH)

    for i in range(7):
        send(i).start()

    for load in loads:
        load.wait()
    ctile = pl.ds(pl.multiple_of(c * TILE, TILE), TILE)
    for k in range(6):
        for l in range(LAYERS):
            gbuf[k, l] = jnp.broadcast_to(mom_ref[k, pl.ds(l, 1), ctile] * (1.0 / 216.0), (16, TILE))
    grad = None
    for k in range(3):
        for l in range(LAYERS):
            at = EDGE + l * PART + k * COLS
            rhs = jnp.concatenate([stage[who, at:at + COLS, :] for who in range(8)], axis=1)
            row = res_ref[k:k + 1, l * PLANE:(l + 1) * PLANE].astype(F32)
            lhs = jnp.broadcast_to(row, (16, PLANE)).astype(BF)
            got = lax.dot_general(lhs, rhs, NT, preferred_element_type=F32)
            grad = got if grad is None else grad + got
    row16 = iota((16, TILE), 0)
    pieces = []
    for l in range(LAYERS):
        x = mis_ref[pl.ds(l, 1), ctile]
        hi = x.astype(BF).astype(F32)
        mid = (x - hi).astype(BF).astype(F32)
        lo = x - hi - mid
        full = jnp.where(row16 == 0, jnp.broadcast_to(hi, (16, TILE)), 0.0)
        full = jnp.where(row16 == 1, jnp.broadcast_to(mid, (16, TILE)), full)
        full = jnp.where(row16 == 2, jnp.broadcast_to(lo, (16, TILE)), full)
        pieces.append(full.astype(BF))
    zone_lhs = jnp.concatenate(pieces, axis=1)
    esrc[0] = jnp.zeros((8, TILE), F32)
    esrc[0, 0:1, 0:COLS] = grad[0:1]
    for half in range(2):
        zone_id = iota((256, TILE), 0) + 256 * half
        hot = jnp.concatenate([
            jnp.where(jnp.broadcast_to(lab_ref[pl.ds(l, 1), ctile], (256, TILE)) == zone_id, 1.0, 0.0).astype(BF)
            for l in range(LAYERS)], axis=1)
        got = lax.dot_general(zone_lhs, hot, NT, preferred_element_type=F32)
        got = got[0:1] + got[1:2] + got[2:3]
        esrc[0, 4 + 2 * half:5 + 2 * half, :] = got[:, 0:TILE]
        esrc[0, 5 + 2 * half:6 + 2 * half, :] = got[:, TILE:2 * TILE]

    small0 = pltpu.make_async_remote_copy(
        src_ref=esrc.at[0], dst_ref=e0, send_sem=es.at[0], recv_sem=er.at[0],
        device_id=(partner, c), device_id_type=MESH)

    def small1(i):
        return pltpu.make_async_remote_copy(
            src_ref=esrc.at[1], dst_ref=e1.at[d], send_sem=es.at[1], recv_sem=er.at[1],
            device_id=(slab_peer(*OFFS[i]), c), device_id_type=MESH)

    def small2(i):
        return pltpu.make_async_remote_copy(
            src_ref=esrc.at[2], dst_ref=e2.at[c], send_sem=es.at[2], recv_sem=er.at[2],
            device_id=(s, col_peer(*OFFS[i])), device_id_type=MESH)

    def wait_all(ref, sem):
        pltpu.make_async_copy(ref, ref, sem).wait()

    small0.start()

    lane = iota((16, TILE), 1)
    not_first = lax.rem(lane, GY) != 0
    inside = lane >= GY
    edge_lane = iota((32, TILE), 1)

    def arrive(j):
        src = order[j]
        wait_all(chunk.at[src], rs.at[src])

        @pl.when(s > 0)
        def _():
            forward(j).start()

    def forward(j):
        src = order[j]
        return pltpu.make_async_remote_copy(
            src_ref=chunk.at[src, pl.ds(0, EDGE + PART), :], dst_ref=above.at[src],
            send_sem=fs.at[j], recv_sem=fz.at[src], device_id=(below, c), device_id_type=MESH)

    def block(j):
        src = order[j]

        @pl.when(s < 15)
        def _():
            wait_all(above.at[src], fz.at[src])

        for k in range(3):
            low = chunk[src, 32 * k:32 * k + 32, :].astype(F32)
            top = above[src, 32 * k:32 * k + 32, :].astype(F32)
            for h in range(2):
                first = low if h == 0 else pltpu.roll(low, 64, 1)
                second = top if h == 1 else pltpu.roll(top, 64, 1)
                both = jnp.where(edge_lane < 64, first, jnp.where(edge_lane < 80, second, 0.0))
                edges[src, COLS * k + 32 * h:COLS * k + 32 * h + 32, :] = both.astype(BF)
        halo = edges[src]
        for l in range(LAYERS + 1):
            if l < LAYERS:
                here = chunk[src, EDGE + l * PART:EDGE + (l + 1) * PART, :]
            else:
                here = above[src, EDGE:EDGE + PART, :]
            got = jnp.dot(jnp.concatenate([here, halo], axis=1), w_ref[l], preferred_element_type=F32)
            fbuf[l] = got.reshape(3, COLS, 4 * TILE)

        @pl.loop(0, COLS // 16)
        def _(r):
            rows = pl.ds(pl.multiple_of(r * 16, 16), 16)
            dest = pl.ds(pl.multiple_of(src * COLS + r * 16, 16), 16)
            carry = [[None] * 3 for _ in range(4)]
            edge = [jnp.zeros((16, TILE), F32) for _ in range(3)]
            for n in range(LAYERS + 1):
                unit = [[None] * 3 for _ in range(4)]
                if n < LAYERS:
                    g = [gbuf[k, n] for k in range(6)]
                    for q in range(4):
                        low, high = [], []
                        for k in range(3):
                            first = fbuf[n, k, rows, q * TILE:(q + 1) * TILE]
                            second = fbuf[n + 1, k, rows, q * TILE:(q + 1) * TILE]
                            both = first + second
                            low.append(first + both)
                            high.append(second + both)

                        def apply(v):
                            return [
                                g[0] * v[0] + g[3] * v[1] + g[4] * v[2],
                                g[3] * v[0] + g[1] * v[1] + g[5] * v[2],
                                g[4] * v[0] + g[5] * v[1] + g[2] * v[2],
                            ]

                        low, high = apply(low), apply(high)
                        for k in range(3):
                            unit[q][k] = low[k] if n == 0 else carry[q][k] + low[k]
                            carry[q][k] = high[k]
                else:
                    unit = carry
                for k in range(3):
                    near = unit[0][k] + jnp.where(not_first, pltpu.roll(unit[1][k], 1, 1), 0.0)
                    far = unit[2][k] + jnp.where(not_first, pltpu.roll(unit[3][k], 1, 1), 0.0)
                    moved = pltpu.roll(far, GY, 1)
                    img[k, dest, n * TILE:(n + 1) * TILE] = (near + jnp.where(inside, moved, 0.0)).astype(BF)
                    if n > 0:
                        moved = pltpu.roll(far, GY * (n + 1), 1)
                    edge[k] = jnp.where((lane >= GY * n) & (lane < GY * (n + 1)), moved, edge[k])
            for k in range(3):
                img[k, dest, KW - TILE:KW] = edge[k].astype(BF)

    arrive(0)
    for j in range(8):
        if j < 7:
            arrive(j + 1)
        block(j)
        if j == 1:
            small0.wait_recv()
            esrc[1] = esrc[0] + e0[...]
            for i in range(7):
                small1(i).start()
            e1[d] = esrc[1]
        if j == 4:
            wait_all(e1.at[pl.ds(0, 7)], er.at[1])
            total = e1[0]
            for who in range(1, 8):
                total = total + e1[who]
            esrc[2] = total
            for i in range(7):
                small2(i).start()
            e2[c] = total

    def panel(half):
        total = None
        for k in range(3):
            rhs = []
            for e in range(8):
                rows = pl.ds(pl.multiple_of(EDGE + k * COLS + half * 32, 32), 32)
                tiles = [
                    chunk[e, pl.ds(pl.multiple_of(EDGE + l * PART + k * COLS + half * 32, 32), 32), :]
                    for l in range(LAYERS)]
                tiles.append(above[e, rows, :])
                tiles.append(edges[e, pl.ds(pl.multiple_of(k * COLS + half * 32, 32), 32), :])
                rhs.append(jnp.concatenate(tiles, axis=1))
            got = lax.dot_general(img[k], jnp.concatenate(rhs, axis=0), NT, preferred_element_type=F32)
            total = got if total is None else total + got
        hacc[half] = total

    other = 1 - core
    panel(other)
    swap = pltpu.make_async_remote_copy(
        src_ref=hacc.at[other], dst_ref=hrecv, send_sem=p0_sem.at[0], recv_sem=p0_sem.at[1],
        device_id=(partner, c), device_id_type=MESH)
    swap.start()
    panel(core)
    swap.wait_recv()

    me = c * 8 + d
    group = lane // 32
    for i in range(8):
        to_c = lax.rem(c + i, 8)
        sums = []
        for g in range(4):
            rows = pl.ds(pl.multiple_of(to_c * COLS + 16 * g, 16), 16)
            sums.append(hacc[core, rows, :] + hrecv[rows, :])
        for e in range(8):
            a, b = e // 4, e % 4
            packed = None
            for g in range(4):
                piece = sums[g][:, a * TILE:(a + 1) * TILE]
                shift = (32 * g - 32 * b) % TILE
                if shift:
                    piece = pltpu.roll(piece, shift, 1)
                packed = piece if packed is None else jnp.where(group == g, piece, packed)
            pack[to_c * 8 + e] = packed
        for j in range(8):
            if i + j == 0:
                continue
            to_d = lax.rem(d + j, 8)
            pltpu.make_async_remote_copy(
                src_ref=pack.at[to_c * 8 + to_d], dst_ref=parts.at[me], send_sem=msem, recv_sem=rsem,
                device_id=(to_d * 2 + core, to_c), device_id_type=MESH).start()
    parts[me] = pack[me]

    wait_all(e2.at[pl.ds(0, 7)], er.at[2])
    zone = e2[0]
    for who in range(1, 8):
        zone = zone + e2[who]
    z_out[...] = zone[4:8] * (WIDTH / 65536)
    left = iota((1, TILE), 1) < COLS
    for t in range(4):
        g_out[t:t + 1, :] = jnp.where(left, e2[2 * t, 0:1, :], pltpu.roll(e2[2 * t + 1, 0:1, :], COLS, 1))

    wait_all(parts.at[pl.ds(0, 63)], rsem)
    total = parts[0]
    for who in range(1, 64):
        total = total + parts[who]
    rows = [pltpu.roll(total, TILE - 32 * g, 1) if g else total for g in range(4)]
    h_out[...] = jnp.transpose(jnp.concatenate(rows, axis=0))[0:32, :]

    @pl.when(s > 0)
    def _():
        for j in range(8):
            forward(j).wait_send()

    for i in range(7):
        send(i).wait_send()
    small0.wait_send()
    wait_all(e1.at[pl.ds(0, 7)], es.at[1])
    wait_all(e2.at[pl.ds(0, 7)], es.at[2])
    swap.wait_send()
    wait_all(parts.at[pl.ds(0, 63)], msem)


def on_device(sensitivity, residual_force, moments, zone_label, misfit):
    any_spec = pl.BlockSpec(memory_space=pl.ANY)
    vmem = pl.BlockSpec(memory_space=pltpu.VMEM)
    dma = pltpu.SemaphoreType.DMA
    h, g, z = pl.pallas_call(
        kernel,
        name="gauss_newton",
        out_shape=(
            jax.ShapeDtypeStruct((32, COLS), F32), jax.ShapeDtypeStruct((4, TILE), F32),
            jax.ShapeDtypeStruct((4, TILE), F32)),
        in_specs=[any_spec] * 5,
        out_specs=(vmem, vmem, vmem),
        scratch_shapes=[
            pltpu.VMEM((LAYERS + 1, 2 * TILE, 4 * TILE), BF),
            pltpu.VMEM((2 * LAYERS * TILE, TILE), BF),
            pltpu.VMEM((3, LAYERS * PLANE), BF),
            pltpu.VMEM((6, LAYERS, PLANE), F32),
            pltpu.VMEM((LAYERS, PLANE), jnp.int32),
            pltpu.VMEM((LAYERS, PLANE), F32),
            pltpu.VMEM((8, CHUNK, TILE), BF),
            pltpu.VMEM((8, CHUNK, TILE), BF),
            pltpu.VMEM((8, EDGE + PART, TILE), BF),
            pltpu.VMEM((8, PART, TILE), BF),
            pltpu.VMEM((3, WIDTH, KW), BF),
            pltpu.VMEM((LAYERS + 1, 3, COLS, 4 * TILE), F32),
            pltpu.VMEM((6, LAYERS, 16, TILE), F32),
            pltpu.VMEM((2, WIDTH, 256), F32),
            pltpu.VMEM((WIDTH, 256), F32),
            pltpu.VMEM((64, 16, TILE), F32),
            pltpu.VMEM((64, 16, TILE), F32),
            pltpu.VMEM((3, 8, TILE), F32),
            pltpu.VMEM((8, TILE), F32),
            pltpu.VMEM((8, 8, TILE), F32),
            pltpu.VMEM((8, 8, TILE), F32),
            dma((4,)), dma((8,)), dma((7,)), dma((8,)), dma((8,)), dma((8,)), dma((2,)),
            dma((3,)), dma((3,)), dma(()), dma(()),
        ],
        compiler_params=pltpu.CompilerParams(collective_id=0, has_side_effects=True, vmem_limit_bytes=67043328),
    )(sensitivity, residual_force, moments, zone_label, misfit)
    return h.T, g.reshape(WIDTH), z.reshape(WIDTH)


def solution(mesh):
    in_specs = (
        P(None, "col", "slab"),
        P(None, "slab"),
        P(None, "slab", None),
        P("slab", None),
        P("slab", None),
    )
    out_specs = (P("col", "slab"), P(), P())
    return jax.shard_map(
        on_device, mesh=mesh, in_specs=in_specs, out_specs=out_specs, check_vma=False
    )
```

```python
import jax
import jax.numpy as jnp
from jax import lax
from jax.experimental import pallas as pl
from jax.experimental.pallas import tpu as pltpu
from jax.sharding import PartitionSpec as P

MESH = pl.DeviceIdType.MESH
GX = 64
GY = 16
PLANE = GX * GY
LAYERS = 4
COLS = 64
WIDTH = 512
TILE = 128
KW = 768
EDGE = 3 * 32
PART = 3 * COLS
CHUNK = EDGE + LAYERS * PART
BF = jnp.bfloat16
F32 = jnp.float32
NT = (((1,), (1,)), ((), ()))
OFFS = ((0, 1), (0, 3), (1, 0), (0, 2), (1, 1), (1, 3), (1, 2))


def iota(shape, dim):
    return lax.broadcasted_iota(jnp.int32, shape, dim)


def pair_weight(shift, side):
    return jnp.where(shift == side, 2.0, jnp.where(shift == 1 - side, 1.0, 0.0))


def fill_pick(pick_ref):
    src, dst = iota((TILE, TILE), 0), iota((TILE, TILE), 1)
    for h in range(2):
        for l in range(LAYERS):
            hit = (src == dst - 64 * h - GY * l) & (src < GY)
            at = (h * LAYERS + l) * TILE
            pick_ref[at:at + TILE, :] = jnp.where(hit, 1.0, 0.0).astype(BF)


def fill_weights(w_ref):
    src, elem = iota((TILE, TILE), 0), iota((TILE, TILE), 1)
    ex, ey = elem // GY, lax.rem(elem, GY)
    sx, sy = src // GY, lax.rem(src, GY)
    for b in range(2):
        for c in range(2):
            wy = pair_weight(sy - ey, c)
            at = (2 * b + c) * TILE
            near = (pair_weight(sx - ex, b) * wy).astype(BF)
            far = pair_weight(8 - ex, b) * wy
            for l in range(LAYERS + 1):
                w_ref[l, 0:TILE, at:at + TILE] = near
                w_ref[l, TILE:2 * TILE, at:at + TILE] = jnp.where(sx == l, far, 0.0).astype(BF)


def kernel(
    s_any, res_any, mom_any, lab_any, mis_any,
    out_ref,
    w_ref, pick_ref, res_ref, mom_ref, lab_ref, mis_ref,
    sloc, hal, chunk, above, edges, img, fbuf, gbuf, hacc, hrecv, pack, parts,
    esrc, e0, e1, e2,
    in_sem, own_sem, sa, sb, ra, rb, fs, fz, p0_sem, es, er, msem, rsem,
):
    s = lax.axis_index("slab")
    c = lax.axis_index("col")
    core = lax.rem(s, 2)
    z = lax.rem(s // 2, 4)
    xh = s // 8
    xl = c // 4
    y = lax.rem(c, 4)
    d = s // 2

    def col_peer(dx, dy):
        return lax.rem(xl + dx, 2) * 4 + lax.rem(y + dy + 4, 4)

    def slab_peer(dx, dz):
        return (lax.rem(xh + dx, 2) * 4 + lax.rem(z + dz + 4, 4)) * 2 + core

    order = [c] + [col_peer(dx, -dy) for dx, dy in OFFS]
    partner = s + 1 - 2 * core
    below = lax.rem(s + 15, 16)
    bar = pltpu.get_barrier_semaphore()
    for k in range(1, 64):
        to_c = lax.rem(c + k // 8, 8)
        to_d = lax.rem(d + k, 8)
        pl.semaphore_signal(bar, inc=1, device_id=(to_d * 2 + core, to_c), device_id_type=MESH)
    for to in (partner, lax.rem(s + 1, 16), below):
        pl.semaphore_signal(bar, inc=1, device_id=(to, c), device_id_type=MESH)

    def wait_all(ref, sem):
        pltpu.make_async_copy(ref, ref, sem).wait()

    def lanes(l, who):
        return pl.ds(pl.multiple_of(l * PLANE + who * TILE, TILE), TILE)

    def tile_rows(l, k):
        return pl.ds(EDGE + l * PART + k * COLS, COLS)

    whole = pltpu.make_async_copy(s_any, sloc, own_sem.at[0])
    whole.start()
    for l in range(LAYERS):
        for k in range(3):
            pltpu.make_async_copy(
                s_any.at[k, :, lanes(l, c)], chunk.at[c, tile_rows(l, k), :], own_sem.at[1]).start()
    loads = [
        pltpu.make_async_copy(a, b, in_sem.at[i])
        for i, (a, b) in enumerate(((res_any, res_ref), (mom_any, mom_ref), (lab_any, lab_ref), (mis_any, mis_ref)))]
    for load in loads:
        load.start()

    @pl.when(s == 15)
    def _():
        above[...] = jnp.zeros_like(above)

    pl.semaphore_wait(bar, 66)

    def send(i, l, sem, to):
        who = col_peer(*OFFS[i])
        for k in range(3):
            pltpu.make_async_remote_copy(
                src_ref=s_any.at[k, :, lanes(l, who)], dst_ref=chunk.at[c, tile_rows(l, k), :],
                send_sem=sem, recv_sem=to.at[c], device_id=(s, who), device_id_type=MESH).start()

    for i in range(7):
        send(i, 0, sa, ra)
    fill_pick(pick_ref)
    whole.wait()
    for who in range(8):
        if who == 7:
            hal[7] = jnp.zeros((EDGE, TILE), BF)
        else:
            tiles = []
            for h in range(2):
                for l in range(LAYERS):
                    at = l * PLANE + (who + 1) * TILE
                    tiles.append(jnp.concatenate(
                        [sloc[k, 32 * h:32 * h + 32, at:at + TILE] for k in range(3)], axis=0))
            got = jnp.dot(jnp.concatenate(tiles, axis=1), pick_ref[...], preferred_element_type=F32)
            hal[who] = got.astype(BF)
    for i in range(7):
        who = col_peer(*OFFS[i])
        pltpu.make_async_remote_copy(
            src_ref=hal.at[who], dst_ref=chunk.at[c, pl.ds(0, EDGE), :],
            send_sem=sa, recv_sem=ra.at[c], device_id=(s, who), device_id_type=MESH).start()
    for i in range(7):
        for l in range(1, LAYERS):
            send(i, l, sb, rb)
    chunk[c, 0:EDGE, :] = hal[c]
    wait_all(chunk.at[c, pl.ds(EDGE, LAYERS * PART), :], own_sem.at[1])

    def forward(j):
        src = order[j]
        return pltpu.make_async_remote_copy(
            src_ref=chunk.at[src, pl.ds(0, EDGE + PART), :], dst_ref=above.at[src],
            send_sem=fs.at[j], recv_sem=fz.at[src], device_id=(below, c), device_id_type=MESH)

    def arrive(j):
        src = order[j]
        if j > 0:
            wait_all(chunk.at[src, pl.ds(0, EDGE + PART), :], ra.at[src])

        @pl.when(s > 0)
        def _():
            forward(j).start()

    arrive(0)
    fill_weights(w_ref)
    for load in loads:
        load.wait()
    ctile = pl.ds(pl.multiple_of(c * TILE, TILE), TILE)
    for k in range(6):
        for l in range(LAYERS):
            gbuf[k, l] = jnp.broadcast_to(mom_ref[k, pl.ds(l, 1), ctile] * (1.0 / 216.0), (16, TILE))
    grad = None
    for k in range(3):
        for l in range(LAYERS):
            rhs = sloc[k, :, l * PLANE:(l + 1) * PLANE]
            row = res_ref[k:k + 1, l * PLANE:(l + 1) * PLANE].astype(F32)
            lhs = jnp.broadcast_to(row, (16, PLANE)).astype(BF)
            got = lax.dot_general(lhs, rhs, NT, preferred_element_type=F32)
            grad = got if grad is None else grad + got
    row16 = iota((16, TILE), 0)
    pieces = []
    for l in range(LAYERS):
        x = mis_ref[pl.ds(l, 1), ctile]
        hi = x.astype(BF).astype(F32)
        mid = (x - hi).astype(BF).astype(F32)
        lo = x - hi - mid
        full = jnp.where(row16 == 0, jnp.broadcast_to(hi, (16, TILE)), 0.0)
        full = jnp.where(row16 == 1, jnp.broadcast_to(mid, (16, TILE)), full)
        full = jnp.where(row16 == 2, jnp.broadcast_to(lo, (16, TILE)), full)
        pieces.append(full.astype(BF))
    zone_lhs = jnp.concatenate(pieces, axis=1)
    esrc[0] = jnp.zeros((8, TILE), F32)
    esrc[0, 0:1, 0:COLS] = grad[0:1]
    for half in range(2):
        zone_id = iota((256, TILE), 0) + 256 * half
        hot = jnp.concatenate([
            jnp.where(jnp.broadcast_to(lab_ref[pl.ds(l, 1), ctile], (256, TILE)) == zone_id, 1.0, 0.0).astype(BF)
            for l in range(LAYERS)], axis=1)
        got = lax.dot_general(zone_lhs, hot, NT, preferred_element_type=F32)
        got = got[0:1] + got[1:2] + got[2:3]
        esrc[0, 4 + 2 * half:5 + 2 * half, :] = got[:, 0:TILE]
        esrc[0, 5 + 2 * half:6 + 2 * half, :] = got[:, TILE:2 * TILE]

    small0 = pltpu.make_async_remote_copy(
        src_ref=esrc.at[0], dst_ref=e0, send_sem=es.at[0], recv_sem=er.at[0],
        device_id=(partner, c), device_id_type=MESH)

    def small1(i):
        return pltpu.make_async_remote_copy(
            src_ref=esrc.at[1], dst_ref=e1.at[d], send_sem=es.at[1], recv_sem=er.at[1],
            device_id=(slab_peer(*OFFS[i]), c), device_id_type=MESH)

    def small2(i):
        return pltpu.make_async_remote_copy(
            src_ref=esrc.at[2], dst_ref=e2.at[c], send_sem=es.at[2], recv_sem=er.at[2],
            device_id=(s, col_peer(*OFFS[i])), device_id_type=MESH)

    small0.start()

    lane = iota((16, TILE), 1)
    not_first = lax.rem(lane, GY) != 0
    inside = lane >= GY
    edge_lane = iota((32, TILE), 1)

    def block(j):
        src = order[j]
        if j > 0:
            wait_all(chunk.at[src, pl.ds(EDGE + PART, 3 * PART), :], rb.at[src])

        @pl.when(s < 15)
        def _():
            wait_all(above.at[src], fz.at[src])

        for k in range(3):
            low = chunk[src, 32 * k:32 * k + 32, :].astype(F32)
            top = above[src, 32 * k:32 * k + 32, :].astype(F32)
            for h in range(2):
                first = low if h == 0 else pltpu.roll(low, 64, 1)
                second = top if h == 1 else pltpu.roll(top, 64, 1)
                both = jnp.where(edge_lane < 64, first, jnp.where(edge_lane < 80, second, 0.0))
                edges[src, COLS * k + 32 * h:COLS * k + 32 * h + 32, :] = both.astype(BF)
        halo = edges[src]
        for l in range(LAYERS + 1):
            if l < LAYERS:
                here = chunk[src, EDGE + l * PART:EDGE + (l + 1) * PART, :]
            else:
                here = above[src, EDGE:EDGE + PART, :]
            got = jnp.dot(jnp.concatenate([here, halo], axis=1), w_ref[l], preferred_element_type=F32)
            fbuf[l] = got.reshape(3, COLS, 4 * TILE)

        @pl.loop(0, COLS // 16)
        def _(r):
            rows = pl.ds(pl.multiple_of(r * 16, 16), 16)
            dest = pl.ds(pl.multiple_of(src * COLS + r * 16, 16), 16)
            carry = [[None] * 3 for _ in range(4)]
            edge = [jnp.zeros((16, TILE), F32) for _ in range(3)]
            for n in range(LAYERS + 1):
                unit = [[None] * 3 for _ in range(4)]
                if n < LAYERS:
                    g = [gbuf[k, n] for k in range(6)]
                    for q in range(4):
                        low, high = [], []
                        for k in range(3):
                            first = fbuf[n, k, rows, q * TILE:(q + 1) * TILE]
                            second = fbuf[n + 1, k, rows, q * TILE:(q + 1) * TILE]
                            both = first + second
                            low.append(first + both)
                            high.append(second + both)

                        def apply(v):
                            return [
                                g[0] * v[0] + g[3] * v[1] + g[4] * v[2],
                                g[3] * v[0] + g[1] * v[1] + g[5] * v[2],
                                g[4] * v[0] + g[5] * v[1] + g[2] * v[2],
                            ]

                        low, high = apply(low), apply(high)
                        for k in range(3):
                            unit[q][k] = low[k] if n == 0 else carry[q][k] + low[k]
                            carry[q][k] = high[k]
                else:
                    unit = carry
                for k in range(3):
                    near = unit[0][k] + jnp.where(not_first, pltpu.roll(unit[1][k], 1, 1), 0.0)
                    far = unit[2][k] + jnp.where(not_first, pltpu.roll(unit[3][k], 1, 1), 0.0)
                    moved = pltpu.roll(far, GY, 1)
                    img[k, dest, n * TILE:(n + 1) * TILE] = (near + jnp.where(inside, moved, 0.0)).astype(BF)
                    if n > 0:
                        moved = pltpu.roll(far, GY * (n + 1), 1)
                    edge[k] = jnp.where((lane >= GY * n) & (lane < GY * (n + 1)), moved, edge[k])
            for k in range(3):
                img[k, dest, KW - TILE:KW] = edge[k].astype(BF)

    for j in range(1, 4):
        arrive(j)
    block(0)
    small0.wait_recv()
    esrc[1] = esrc[0] + e0[...]
    for i in range(7):
        small1(i).start()
    e1[d] = esrc[1]
    for j in range(4, 8):
        arrive(j)
    for j in range(1, 8):
        block(j)

    def panel(half):
        total = None
        for k in range(3):
            rhs = []
            for e in range(8):
                rows = pl.ds(pl.multiple_of(EDGE + k * COLS + half * 32, 32), 32)
                tiles = [
                    chunk[e, pl.ds(pl.multiple_of(EDGE + l * PART + k * COLS + half * 32, 32), 32), :]
                    for l in range(LAYERS)]
                tiles.append(above[e, rows, :])
                tiles.append(edges[e, pl.ds(pl.multiple_of(k * COLS + half * 32, 32), 32), :])
                rhs.append(jnp.concatenate(tiles, axis=1))
            got = lax.dot_general(img[k], jnp.concatenate(rhs, axis=0), NT, preferred_element_type=F32)
            total = got if total is None else total + got
        hacc[half] = total

    other = 1 - core
    panel(other)
    swap = pltpu.make_async_remote_copy(
        src_ref=hacc.at[other], dst_ref=hrecv, send_sem=p0_sem.at[0], recv_sem=p0_sem.at[1],
        device_id=(partner, c), device_id_type=MESH)
    swap.start()
    wait_all(e1.at[pl.ds(0, 7)], er.at[1])
    total = e1[0]
    for who in range(1, 8):
        total = total + e1[who]
    esrc[2] = total
    for i in range(7):
        small2(i).start()
    e2[c] = total
    panel(core)
    swap.wait_recv()

    me = c * 8 + d
    group = lane // 32
    for i in range(8):
        to_c = lax.rem(c + i, 8)
        sums = []
        for g in range(4):
            rows = pl.ds(pl.multiple_of(to_c * COLS + 16 * g, 16), 16)
            sums.append(hacc[core, rows, :] + hrecv[rows, :])
        for e in range(8):
            a, b = e // 4, e % 4
            packed = None
            for g in range(4):
                piece = sums[g][:, a * TILE:(a + 1) * TILE]
                shift = (32 * g - 32 * b) % TILE
                if shift:
                    piece = pltpu.roll(piece, shift, 1)
                packed = piece if packed is None else jnp.where(group == g, piece, packed)
            pack[to_c * 8 + e] = packed
        for j in range(8):
            if i + j == 0:
                continue
            to_d = lax.rem(d + j, 8)
            pltpu.make_async_remote_copy(
                src_ref=pack.at[to_c * 8 + to_d], dst_ref=parts.at[me], send_sem=msem, recv_sem=rsem,
                device_id=(to_d * 2 + core, to_c), device_id_type=MESH).start()
    parts[me] = pack[me]

    wait_all(e2.at[pl.ds(0, 7)], er.at[2])
    zone = e2[0]
    for who in range(1, 8):
        zone = zone + e2[who]
    out_ref[36:40, :] = zone[4:8] * (WIDTH / 65536)
    left = iota((1, TILE), 1) < COLS
    for t in range(4):
        out_ref[32 + t:33 + t, :] = jnp.where(left, e2[2 * t, 0:1, :], pltpu.roll(e2[2 * t + 1, 0:1, :], COLS, 1))

    wait_all(parts.at[pl.ds(0, 63)], rsem)
    total = parts[0]
    for who in range(1, 64):
        total = total + parts[who]
    rows = [pltpu.roll(total, TILE - 32 * g, 1) if g else total for g in range(4)]
    out_ref[0:32, 0:COLS] = jnp.transpose(jnp.concatenate(rows, axis=0))[0:32, :]

    @pl.when(s > 0)
    def _():
        for j in range(8):
            forward(j).wait_send()

    wait_all(chunk.at[pl.ds(0, 7), pl.ds(0, EDGE + PART), :], sa)
    wait_all(chunk.at[pl.ds(0, 7), pl.ds(EDGE + PART, 3 * PART), :], sb)
    small0.wait_send()
    wait_all(e1.at[pl.ds(0, 7)], es.at[1])
    wait_all(e2.at[pl.ds(0, 7)], es.at[2])
    swap.wait_send()
    wait_all(parts.at[pl.ds(0, 63)], msem)


def on_device(sensitivity, residual_force, moments, zone_label, misfit):
    any_spec = pl.BlockSpec(memory_space=pl.ANY)
    vmem = pl.BlockSpec(memory_space=pltpu.VMEM)
    dma = pltpu.SemaphoreType.DMA
    out = pl.pallas_call(
        kernel,
        name="gauss_newton",
        out_shape=jax.ShapeDtypeStruct((40, TILE), F32),
        in_specs=[any_spec] * 5,
        out_specs=vmem,
        scratch_shapes=[
            pltpu.VMEM((LAYERS + 1, 2 * TILE, 4 * TILE), BF),
            pltpu.VMEM((2 * LAYERS * TILE, TILE), BF),
            pltpu.VMEM((3, LAYERS * PLANE), BF),
            pltpu.VMEM((6, LAYERS, PLANE), F32),
            pltpu.VMEM((LAYERS, PLANE), jnp.int32),
            pltpu.VMEM((LAYERS, PLANE), F32),
            pltpu.VMEM((3, COLS, LAYERS * PLANE), BF),
            pltpu.VMEM((8, EDGE, TILE), BF),
            pltpu.VMEM((8, CHUNK, TILE), BF),
            pltpu.VMEM((8, EDGE + PART, TILE), BF),
            pltpu.VMEM((8, PART, TILE), BF),
            pltpu.VMEM((3, WIDTH, KW), BF),
            pltpu.VMEM((LAYERS + 1, 3, COLS, 4 * TILE), F32),
            pltpu.VMEM((6, LAYERS, 16, TILE), F32),
            pltpu.VMEM((2, WIDTH, 256), F32),
            pltpu.VMEM((WIDTH, 256), F32),
            pltpu.VMEM((64, 16, TILE), F32),
            pltpu.VMEM((64, 16, TILE), F32),
            pltpu.VMEM((3, 8, TILE), F32),
            pltpu.VMEM((8, TILE), F32),
            pltpu.VMEM((8, 8, TILE), F32),
            pltpu.VMEM((8, 8, TILE), F32),
            dma((4,)), dma((2,)), dma(()), dma(()), dma((8,)), dma((8,)), dma((8,)), dma((8,)), dma((2,)),
            dma((3,)), dma((3,)), dma(()), dma(()),
        ],
        compiler_params=pltpu.CompilerParams(collective_id=0, has_side_effects=True, vmem_limit_bytes=67043328),
    )(sensitivity, residual_force, moments, zone_label, misfit)
    return out[0:32, 0:COLS].T, out[32:36].reshape(WIDTH), out[36:40].reshape(WIDTH)


def solution(mesh):
    in_specs = (
        P(None, "col", "slab"),
        P(None, "slab"),
        P(None, "slab", None),
        P("slab", None),
        P("slab", None),
    )
    out_specs = (P("col", "slab"), P(), P())
    return jax.shard_map(
        on_device, mesh=mesh, in_specs=in_specs, out_specs=out_specs, check_vma=False
    )
```

```python
import jax
import jax.numpy as jnp
from jax import lax
from jax.experimental import pallas as pl
from jax.experimental.pallas import tpu as pltpu
from jax.sharding import PartitionSpec as P

MESH = pl.DeviceIdType.MESH
GX = 64
GY = 16
PLANE = GX * GY
LAYERS = 4
COLS = 64
WIDTH = 512
TILE = 128
KW = 768
EDGE = 3 * 32
PART = 3 * COLS
CHUNK = EDGE + LAYERS * PART
BF = jnp.bfloat16
F32 = jnp.float32
NT = (((1,), (1,)), ((), ()))
OFFS = ((0, 1), (0, 3), (1, 0), (0, 2), (1, 1), (1, 3), (1, 2))


def iota(shape, dim):
    return lax.broadcasted_iota(jnp.int32, shape, dim)


def pair_weight(shift, side):
    return jnp.where(shift == side, 2.0, jnp.where(shift == 1 - side, 1.0, 0.0))


def fill_pick(pick_ref):
    src, dst = iota((TILE, TILE), 0), iota((TILE, TILE), 1)
    for h in range(2):
        for l in range(LAYERS):
            hit = (src == dst - 64 * h - GY * l) & (src < GY)
            at = (h * LAYERS + l) * TILE
            pick_ref[at:at + TILE, :] = jnp.where(hit, 1.0, 0.0).astype(BF)


def fill_weights(w_ref):
    src, elem = iota((TILE, TILE), 0), iota((TILE, TILE), 1)
    ex, ey = elem // GY, lax.rem(elem, GY)
    sx, sy = src // GY, lax.rem(src, GY)
    for b in range(2):
        for c in range(2):
            wy = pair_weight(sy - ey, c)
            at = (2 * b + c) * TILE
            near = (pair_weight(sx - ex, b) * wy).astype(BF)
            far = pair_weight(8 - ex, b) * wy
            for l in range(LAYERS + 1):
                w_ref[l, 0:TILE, at:at + TILE] = near
                w_ref[l, TILE:2 * TILE, at:at + TILE] = jnp.where(sx == l, far, 0.0).astype(BF)


def kernel(
    s_any, res_any, mom_any, lab_any, mis_any,
    out_ref,
    w_ref, pick_ref, res_ref, mom_ref, lab_ref, mis_ref,
    sloc, hal, chunk, above, edges, img, fbuf, gbuf, hacc, hrecv, pack, parts,
    esrc, e0, e1, e2,
    in_sem, own_sem, sa, sb, ra, rb, fs, fz, p0_sem, p1_sem, es, er, msem, rsem,
):
    s = lax.axis_index("slab")
    c = lax.axis_index("col")
    core = lax.rem(s, 2)
    z = lax.rem(s // 2, 4)
    xh = s // 8
    xl = c // 4
    y = lax.rem(c, 4)
    d = s // 2

    def col_peer(dx, dy):
        return lax.rem(xl + dx, 2) * 4 + lax.rem(y + dy + 4, 4)

    def slab_peer(dx, dz):
        return (lax.rem(xh + dx, 2) * 4 + lax.rem(z + dz + 4, 4)) * 2 + core

    order = [c] + [col_peer(dx, -dy) for dx, dy in OFFS]
    partner = s + 1 - 2 * core
    below = lax.rem(s + 15, 16)
    bar = pltpu.get_barrier_semaphore()
    for k in range(1, 64):
        to_c = lax.rem(c + k // 8, 8)
        to_d = lax.rem(d + k, 8)
        pl.semaphore_signal(bar, inc=1, device_id=(to_d * 2 + core, to_c), device_id_type=MESH)
    for to in (partner, lax.rem(s + 1, 16), below):
        pl.semaphore_signal(bar, inc=1, device_id=(to, c), device_id_type=MESH)

    def wait_all(ref, sem):
        pltpu.make_async_copy(ref, ref, sem).wait()

    def lanes(l, who):
        return pl.ds(pl.multiple_of(l * PLANE + who * TILE, TILE), TILE)

    def tile_rows(l, k):
        return pl.ds(EDGE + l * PART + k * COLS, COLS)

    whole = pltpu.make_async_copy(s_any, sloc, own_sem.at[0])
    whole.start()
    for l in range(LAYERS):
        for k in range(3):
            pltpu.make_async_copy(
                s_any.at[k, :, lanes(l, c)], chunk.at[c, tile_rows(l, k), :], own_sem.at[1]).start()
    loads = [
        pltpu.make_async_copy(a, b, in_sem.at[i])
        for i, (a, b) in enumerate(((res_any, res_ref), (mom_any, mom_ref), (lab_any, lab_ref), (mis_any, mis_ref)))]
    for load in loads:
        load.start()

    @pl.when(s == 15)
    def _():
        above[...] = jnp.zeros_like(above)

    pl.semaphore_wait(bar, 66)

    def send(i, l, sem, to):
        who = col_peer(*OFFS[i])
        for k in range(3):
            pltpu.make_async_remote_copy(
                src_ref=s_any.at[k, :, lanes(l, who)], dst_ref=chunk.at[c, tile_rows(l, k), :],
                send_sem=sem, recv_sem=to.at[c], device_id=(s, who), device_id_type=MESH).start()

    for i in range(7):
        send(i, 0, sa, ra)
    fill_pick(pick_ref)
    whole.wait()
    for who in range(8):
        if who == 7:
            hal[7] = jnp.zeros((EDGE, TILE), BF)
        else:
            tiles = []
            for h in range(2):
                for l in range(LAYERS):
                    at = l * PLANE + (who + 1) * TILE
                    tiles.append(jnp.concatenate(
                        [sloc[k, 32 * h:32 * h + 32, at:at + TILE] for k in range(3)], axis=0))
            got = jnp.dot(jnp.concatenate(tiles, axis=1), pick_ref[...], preferred_element_type=F32)
            hal[who] = got.astype(BF)
    for i in range(7):
        who = col_peer(*OFFS[i])
        pltpu.make_async_remote_copy(
            src_ref=hal.at[who], dst_ref=chunk.at[c, pl.ds(0, EDGE), :],
            send_sem=sa, recv_sem=ra.at[c], device_id=(s, who), device_id_type=MESH).start()
    chunk[c, 0:EDGE, :] = hal[c]
    wait_all(chunk.at[c, pl.ds(EDGE, LAYERS * PART), :], own_sem.at[1])

    def forward(j):
        src = order[j]
        return pltpu.make_async_remote_copy(
            src_ref=chunk.at[src, pl.ds(0, EDGE + PART), :], dst_ref=above.at[src],
            send_sem=fs.at[j], recv_sem=fz.at[src], device_id=(below, c), device_id_type=MESH)

    def arrive(j):
        src = order[j]
        if j > 0:
            wait_all(chunk.at[src, pl.ds(0, EDGE + PART), :], ra.at[src])

        @pl.when(s > 0)
        def _():
            forward(j).start()

    arrive(0)
    fill_weights(w_ref)
    for load in loads:
        load.wait()
    ctile = pl.ds(pl.multiple_of(c * TILE, TILE), TILE)
    for k in range(6):
        for l in range(LAYERS):
            gbuf[k, l] = jnp.broadcast_to(mom_ref[k, pl.ds(l, 1), ctile] * (1.0 / 216.0), (16, TILE))
    grad = None
    for k in range(3):
        for l in range(LAYERS):
            rhs = sloc[k, :, l * PLANE:(l + 1) * PLANE]
            row = res_ref[k:k + 1, l * PLANE:(l + 1) * PLANE].astype(F32)
            lhs = jnp.broadcast_to(row, (16, PLANE)).astype(BF)
            got = lax.dot_general(lhs, rhs, NT, preferred_element_type=F32)
            grad = got if grad is None else grad + got
    row16 = iota((16, TILE), 0)
    pieces = []
    for l in range(LAYERS):
        x = mis_ref[pl.ds(l, 1), ctile]
        hi = x.astype(BF).astype(F32)
        mid = (x - hi).astype(BF).astype(F32)
        lo = x - hi - mid
        full = jnp.where(row16 == 0, jnp.broadcast_to(hi, (16, TILE)), 0.0)
        full = jnp.where(row16 == 1, jnp.broadcast_to(mid, (16, TILE)), full)
        full = jnp.where(row16 == 2, jnp.broadcast_to(lo, (16, TILE)), full)
        pieces.append(full.astype(BF))
    zone_lhs = jnp.concatenate(pieces, axis=1)
    esrc[0] = jnp.zeros((8, TILE), F32)
    esrc[0, 0:1, 0:COLS] = grad[0:1]
    for half in range(2):
        zone_id = iota((256, TILE), 0) + 256 * half
        hot = jnp.concatenate([
            jnp.where(jnp.broadcast_to(lab_ref[pl.ds(l, 1), ctile], (256, TILE)) == zone_id, 1.0, 0.0).astype(BF)
            for l in range(LAYERS)], axis=1)
        got = lax.dot_general(zone_lhs, hot, NT, preferred_element_type=F32)
        got = got[0:1] + got[1:2] + got[2:3]
        esrc[0, 4 + 2 * half:5 + 2 * half, :] = got[:, 0:TILE]
        esrc[0, 5 + 2 * half:6 + 2 * half, :] = got[:, TILE:2 * TILE]

    small0 = pltpu.make_async_remote_copy(
        src_ref=esrc.at[0], dst_ref=e0, send_sem=es.at[0], recv_sem=er.at[0],
        device_id=(partner, c), device_id_type=MESH)

    def small1(i):
        return pltpu.make_async_remote_copy(
            src_ref=esrc.at[1], dst_ref=e1.at[d], send_sem=es.at[1], recv_sem=er.at[1],
            device_id=(slab_peer(*OFFS[i]), c), device_id_type=MESH)

    def small2(i):
        return pltpu.make_async_remote_copy(
            src_ref=esrc.at[2], dst_ref=e2.at[c], send_sem=es.at[2], recv_sem=er.at[2],
            device_id=(s, col_peer(*OFFS[i])), device_id_type=MESH)

    small0.start()

    lane = iota((16, TILE), 1)
    not_first = lax.rem(lane, GY) != 0
    inside = lane >= GY
    edge_lane = iota((32, TILE), 1)

    def block(j):
        src = order[j]
        if j > 0:
            wait_all(chunk.at[src, pl.ds(EDGE + PART, 3 * PART), :], rb.at[src])

        @pl.when(s < 15)
        def _():
            wait_all(above.at[src], fz.at[src])

        for k in range(3):
            low = chunk[src, 32 * k:32 * k + 32, :].astype(F32)
            top = above[src, 32 * k:32 * k + 32, :].astype(F32)
            for h in range(2):
                first = low if h == 0 else pltpu.roll(low, 64, 1)
                second = top if h == 1 else pltpu.roll(top, 64, 1)
                both = jnp.where(edge_lane < 64, first, jnp.where(edge_lane < 80, second, 0.0))
                edges[src, COLS * k + 32 * h:COLS * k + 32 * h + 32, :] = both.astype(BF)
        halo = edges[src]
        for l in range(LAYERS + 1):
            if l < LAYERS:
                here = chunk[src, EDGE + l * PART:EDGE + (l + 1) * PART, :]
            else:
                here = above[src, EDGE:EDGE + PART, :]
            got = jnp.dot(jnp.concatenate([here, halo], axis=1), w_ref[l], preferred_element_type=F32)
            fbuf[l] = got.reshape(3, COLS, 4 * TILE)

        @pl.loop(0, COLS // 16)
        def _(r):
            rows = pl.ds(pl.multiple_of(r * 16, 16), 16)
            dest = pl.ds(pl.multiple_of(src * COLS + r * 16, 16), 16)
            carry = [[None] * 3 for _ in range(4)]
            edge = [jnp.zeros((16, TILE), F32) for _ in range(3)]
            for n in range(LAYERS + 1):
                unit = [[None] * 3 for _ in range(4)]
                if n < LAYERS:
                    g = [gbuf[k, n] for k in range(6)]
                    for q in range(4):
                        low, high = [], []
                        for k in range(3):
                            first = fbuf[n, k, rows, q * TILE:(q + 1) * TILE]
                            second = fbuf[n + 1, k, rows, q * TILE:(q + 1) * TILE]
                            both = first + second
                            low.append(first + both)
                            high.append(second + both)

                        def apply(v):
                            return [
                                g[0] * v[0] + g[3] * v[1] + g[4] * v[2],
                                g[3] * v[0] + g[1] * v[1] + g[5] * v[2],
                                g[4] * v[0] + g[5] * v[1] + g[2] * v[2],
                            ]

                        low, high = apply(low), apply(high)
                        for k in range(3):
                            unit[q][k] = low[k] if n == 0 else carry[q][k] + low[k]
                            carry[q][k] = high[k]
                else:
                    unit = carry
                for k in range(3):
                    near = unit[0][k] + jnp.where(not_first, pltpu.roll(unit[1][k], 1, 1), 0.0)
                    far = unit[2][k] + jnp.where(not_first, pltpu.roll(unit[3][k], 1, 1), 0.0)
                    moved = pltpu.roll(far, GY, 1)
                    img[k, dest, n * TILE:(n + 1) * TILE] = (near + jnp.where(inside, moved, 0.0)).astype(BF)
                    if n > 0:
                        moved = pltpu.roll(far, GY * (n + 1), 1)
                    edge[k] = jnp.where((lane >= GY * n) & (lane < GY * (n + 1)), moved, edge[k])
            for k in range(3):
                img[k, dest, KW - TILE:KW] = edge[k].astype(BF)

    wait_all(chunk.at[pl.ds(0, 7), pl.ds(0, EDGE + PART), :], sa)
    for i in range(3):
        for l in range(1, LAYERS):
            send(i, l, sb, rb)
    for j in range(1, 4):
        arrive(j)
    block(0)
    wait_all(chunk.at[pl.ds(0, 3), pl.ds(EDGE + PART, 3 * PART), :], sb)
    for i in range(3, 7):
        for l in range(1, LAYERS):
            send(i, l, sb, rb)
    small0.wait_recv()
    esrc[1] = esrc[0] + e0[...]
    for i in range(7):
        small1(i).start()
    e1[d] = esrc[1]
    for j in range(4, 8):
        arrive(j)
    for j in range(1, 8):
        block(j)

    def panel(half):
        total = None
        for k in range(3):
            rhs = []
            for e in range(8):
                rows = pl.ds(pl.multiple_of(EDGE + k * COLS + half * 32, 32), 32)
                tiles = [
                    chunk[e, pl.ds(pl.multiple_of(EDGE + l * PART + k * COLS + half * 32, 32), 32), :]
                    for l in range(LAYERS)]
                tiles.append(above[e, rows, :])
                tiles.append(edges[e, pl.ds(pl.multiple_of(k * COLS + half * 32, 32), 32), :])
                rhs.append(jnp.concatenate(tiles, axis=1))
            got = lax.dot_general(img[k], jnp.concatenate(rhs, axis=0), NT, preferred_element_type=F32)
            total = got if total is None else total + got
        hacc[half] = total

    other = 1 - core
    panel(other)
    def swap(i):
        rows = pl.ds(pl.multiple_of(lax.rem(c + i, 8) * COLS, COLS), COLS)
        return pltpu.make_async_remote_copy(
            src_ref=hacc.at[other, rows, :], dst_ref=hrecv.at[rows, :], send_sem=p0_sem.at[i], recv_sem=p1_sem.at[i],
            device_id=(partner, c), device_id_type=MESH)

    for i in range(8):
        swap(i).start()
    wait_all(e1.at[pl.ds(0, 7)], er.at[1])
    total = e1[0]
    for who in range(1, 8):
        total = total + e1[who]
    esrc[2] = total
    for i in range(7):
        small2(i).start()
    e2[c] = total
    panel(core)

    me = c * 8 + d
    group = lane // 32
    for i in range(8):
        to_c = lax.rem(c + i, 8)
        swap(i).wait_recv()
        sums = []
        for g in range(4):
            rows = pl.ds(pl.multiple_of(to_c * COLS + 16 * g, 16), 16)
            sums.append(hacc[core, rows, :] + hrecv[rows, :])
        for e in range(8):
            a, b = e // 4, e % 4
            packed = None
            for g in range(4):
                piece = sums[g][:, a * TILE:(a + 1) * TILE]
                shift = (32 * g - 32 * b) % TILE
                if shift:
                    piece = pltpu.roll(piece, shift, 1)
                packed = piece if packed is None else jnp.where(group == g, piece, packed)
            pack[to_c * 8 + e] = packed
        for j in range(8):
            if i + j == 0:
                continue
            to_d = lax.rem(d + j, 8)
            pltpu.make_async_remote_copy(
                src_ref=pack.at[to_c * 8 + to_d], dst_ref=parts.at[me], send_sem=msem, recv_sem=rsem,
                device_id=(to_d * 2 + core, to_c), device_id_type=MESH).start()
    parts[me] = pack[me]

    wait_all(e2.at[pl.ds(0, 7)], er.at[2])
    zone = e2[0]
    for who in range(1, 8):
        zone = zone + e2[who]
    out_ref[36:40, :] = zone[4:8] * (WIDTH / 65536)
    left = iota((1, TILE), 1) < COLS
    for t in range(4):
        out_ref[32 + t:33 + t, :] = jnp.where(left, e2[2 * t, 0:1, :], pltpu.roll(e2[2 * t + 1, 0:1, :], COLS, 1))

    wait_all(parts.at[pl.ds(0, 63)], rsem)
    total = parts[0]
    for who in range(1, 64):
        total = total + parts[who]
    rows = [pltpu.roll(total, TILE - 32 * g, 1) if g else total for g in range(4)]
    out_ref[0:32, 0:COLS] = jnp.transpose(jnp.concatenate(rows, axis=0))[0:32, :]

    @pl.when(s > 0)
    def _():
        for j in range(8):
            forward(j).wait_send()

    wait_all(chunk.at[pl.ds(0, 4), pl.ds(EDGE + PART, 3 * PART), :], sb)
    small0.wait_send()
    wait_all(e1.at[pl.ds(0, 7)], es.at[1])
    wait_all(e2.at[pl.ds(0, 7)], es.at[2])
    for i in range(8):
        swap(i).wait_send()
    wait_all(parts.at[pl.ds(0, 63)], msem)


def on_device(sensitivity, residual_force, moments, zone_label, misfit):
    any_spec = pl.BlockSpec(memory_space=pl.ANY)
    vmem = pl.BlockSpec(memory_space=pltpu.VMEM)
    dma = pltpu.SemaphoreType.DMA
    out = pl.pallas_call(
        kernel,
        name="gauss_newton",
        out_shape=jax.ShapeDtypeStruct((40, TILE), F32),
        in_specs=[any_spec] * 5,
        out_specs=vmem,
        scratch_shapes=[
            pltpu.VMEM((LAYERS + 1, 2 * TILE, 4 * TILE), BF),
            pltpu.VMEM((2 * LAYERS * TILE, TILE), BF),
            pltpu.VMEM((3, LAYERS * PLANE), BF),
            pltpu.VMEM((6, LAYERS, PLANE), F32),
            pltpu.VMEM((LAYERS, PLANE), jnp.int32),
            pltpu.VMEM((LAYERS, PLANE), F32),
            pltpu.VMEM((3, COLS, LAYERS * PLANE), BF),
            pltpu.VMEM((8, EDGE, TILE), BF),
            pltpu.VMEM((8, CHUNK, TILE), BF),
            pltpu.VMEM((8, EDGE + PART, TILE), BF),
            pltpu.VMEM((8, PART, TILE), BF),
            pltpu.VMEM((3, WIDTH, KW), BF),
            pltpu.VMEM((LAYERS + 1, 3, COLS, 4 * TILE), F32),
            pltpu.VMEM((6, LAYERS, 16, TILE), F32),
            pltpu.VMEM((2, WIDTH, 256), F32),
            pltpu.VMEM((WIDTH, 256), F32),
            pltpu.VMEM((64, 16, TILE), F32),
            pltpu.VMEM((64, 16, TILE), F32),
            pltpu.VMEM((3, 8, TILE), F32),
            pltpu.VMEM((8, TILE), F32),
            pltpu.VMEM((8, 8, TILE), F32),
            pltpu.VMEM((8, 8, TILE), F32),
            dma((4,)), dma((2,)), dma(()), dma(()), dma((8,)), dma((8,)), dma((8,)), dma((8,)), dma((8,)), dma((8,)),
            dma((3,)), dma((3,)), dma(()), dma(()),
        ],
        compiler_params=pltpu.CompilerParams(collective_id=0, has_side_effects=True, vmem_limit_bytes=67043328),
    )(sensitivity, residual_force, moments, zone_label, misfit)
    return out[0:32, 0:COLS].T, out[32:36].reshape(WIDTH), out[36:40].reshape(WIDTH)


def solution(mesh):
    in_specs = (
        P(None, "col", "slab"),
        P(None, "slab"),
        P(None, "slab", None),
        P("slab", None),
        P("slab", None),
    )
    out_specs = (P("col", "slab"), P(), P())
    return jax.shard_map(
        on_device, mesh=mesh, in_specs=in_specs, out_specs=out_specs, check_vma=False
    )
```

```python
import jax
import jax.numpy as jnp
from jax import lax
from jax.experimental import pallas as pl
from jax.experimental.pallas import tpu as pltpu
from jax.sharding import PartitionSpec as P

MESH = pl.DeviceIdType.MESH
GX = 64
GY = 16
PLANE = GX * GY
LAYERS = 4
COLS = 64
WIDTH = 512
TILE = 128
KW = 768
EDGE = 3 * 32
PART = 3 * COLS
CHUNK = EDGE + LAYERS * PART
BF = jnp.bfloat16
F32 = jnp.float32
NT = (((1,), (1,)), ((), ()))
OFFS = ((0, 1), (0, 3), (1, 0), (0, 2), (1, 1), (1, 3), (1, 2))


def iota(shape, dim):
    return lax.broadcasted_iota(jnp.int32, shape, dim)


def pair_weight(shift, side):
    return jnp.where(shift == side, 2.0, jnp.where(shift == 1 - side, 1.0, 0.0))


def fill_pick(pick_ref):
    src, dst = iota((TILE, TILE), 0), iota((TILE, TILE), 1)
    for h in range(2):
        for l in range(LAYERS):
            hit = (src == dst - 64 * h - GY * l) & (src < GY)
            at = (h * LAYERS + l) * TILE
            pick_ref[at:at + TILE, :] = jnp.where(hit, 1.0, 0.0).astype(BF)


def fill_weights(w_ref):
    src, elem = iota((TILE, TILE), 0), iota((TILE, TILE), 1)
    ex, ey = elem // GY, lax.rem(elem, GY)
    sx, sy = src // GY, lax.rem(src, GY)
    for b in range(2):
        for c in range(2):
            wy = pair_weight(sy - ey, c)
            at = (2 * b + c) * TILE
            near = (pair_weight(sx - ex, b) * wy).astype(BF)
            far = pair_weight(8 - ex, b) * wy
            for l in range(LAYERS + 1):
                w_ref[l, 0:TILE, at:at + TILE] = near
                w_ref[l, TILE:2 * TILE, at:at + TILE] = jnp.where(sx == l, far, 0.0).astype(BF)


def kernel(
    s_any, res_any, mom_any, lab_any, mis_any,
    out_ref,
    w_ref, pick_ref, res_ref, mom_ref, lab_ref, mis_ref,
    sloc, hal, chunk, above, edges, img, fbuf, gbuf, hacc, hrecv, pack, parts,
    esrc, e0, e1, e2,
    in_sem, own_sem, sa, sb, ra, rb, fs, fz, p0_sem, p1_sem, es, er, msem, rsem,
):
    s = lax.axis_index("slab")
    c = lax.axis_index("col")
    core = lax.rem(s, 2)
    z = lax.rem(s // 2, 4)
    xh = s // 8
    xl = c // 4
    y = lax.rem(c, 4)
    d = s // 2

    def col_peer(dx, dy):
        return lax.rem(xl + dx, 2) * 4 + lax.rem(y + dy + 4, 4)

    def slab_peer(dx, dz):
        return (lax.rem(xh + dx, 2) * 4 + lax.rem(z + dz + 4, 4)) * 2 + core

    order = [c] + [col_peer(dx, -dy) for dx, dy in OFFS]
    partner = s + 1 - 2 * core
    below = lax.rem(s + 15, 16)
    bar = pltpu.get_barrier_semaphore()
    for dx, dy in OFFS:
        pl.semaphore_signal(bar, inc=1, device_id=(s, col_peer(dx, dy)), device_id_type=MESH)
        pl.semaphore_signal(bar, inc=1, device_id=(slab_peer(dx, dy), c), device_id_type=MESH)
    for to in (partner, lax.rem(s + 1, 16), below):
        pl.semaphore_signal(bar, inc=1, device_id=(to, c), device_id_type=MESH)

    def wait_all(ref, sem):
        pltpu.make_async_copy(ref, ref, sem).wait()

    def lanes(l, who):
        return pl.ds(pl.multiple_of(l * PLANE + who * TILE, TILE), TILE)

    def tile_rows(l, k):
        return pl.ds(EDGE + l * PART + k * COLS, COLS)

    whole = pltpu.make_async_copy(s_any, sloc, own_sem.at[0])
    whole.start()
    for l in range(LAYERS):
        for k in range(3):
            pltpu.make_async_copy(
                s_any.at[k, :, lanes(l, c)], chunk.at[c, tile_rows(l, k), :], own_sem.at[1]).start()
    loads = [
        pltpu.make_async_copy(a, b, in_sem.at[i])
        for i, (a, b) in enumerate(((res_any, res_ref), (mom_any, mom_ref), (lab_any, lab_ref), (mis_any, mis_ref)))]
    for load in loads:
        load.start()

    @pl.when(s == 15)
    def _():
        above[...] = jnp.zeros_like(above)

    pl.semaphore_wait(bar, 17)

    def send(i, l, sem, to):
        who = col_peer(*OFFS[i])
        for k in range(3):
            pltpu.make_async_remote_copy(
                src_ref=s_any.at[k, :, lanes(l, who)], dst_ref=chunk.at[c, tile_rows(l, k), :],
                send_sem=sem, recv_sem=to.at[c], device_id=(s, who), device_id_type=MESH).start()

    for i in range(7):
        send(i, 0, sa, ra)
    fill_pick(pick_ref)
    whole.wait()
    for who in range(8):
        if who == 7:
            hal[7] = jnp.zeros((EDGE, TILE), BF)
        else:
            tiles = []
            for h in range(2):
                for l in range(LAYERS):
                    at = l * PLANE + (who + 1) * TILE
                    tiles.append(jnp.concatenate(
                        [sloc[k, 32 * h:32 * h + 32, at:at + TILE] for k in range(3)], axis=0))
            got = jnp.dot(jnp.concatenate(tiles, axis=1), pick_ref[...], preferred_element_type=F32)
            hal[who] = got.astype(BF)
    for i in range(7):
        who = col_peer(*OFFS[i])
        pltpu.make_async_remote_copy(
            src_ref=hal.at[who], dst_ref=chunk.at[c, pl.ds(0, EDGE), :],
            send_sem=sa, recv_sem=ra.at[c], device_id=(s, who), device_id_type=MESH).start()
    chunk[c, 0:EDGE, :] = hal[c]
    wait_all(chunk.at[c, pl.ds(EDGE, LAYERS * PART), :], own_sem.at[1])

    def forward(j):
        src = order[j]
        return pltpu.make_async_remote_copy(
            src_ref=chunk.at[src, pl.ds(0, EDGE + PART), :], dst_ref=above.at[src],
            send_sem=fs.at[j], recv_sem=fz.at[src], device_id=(below, c), device_id_type=MESH)

    def arrive(j):
        src = order[j]
        if j > 0:
            wait_all(chunk.at[src, pl.ds(0, EDGE + PART), :], ra.at[src])

        @pl.when(s > 0)
        def _():
            forward(j).start()

    arrive(0)
    fill_weights(w_ref)
    for load in loads:
        load.wait()
    ctile = pl.ds(pl.multiple_of(c * TILE, TILE), TILE)
    for k in range(6):
        for l in range(LAYERS):
            gbuf[k, l] = jnp.broadcast_to(mom_ref[k, pl.ds(l, 1), ctile] * (1.0 / 216.0), (16, TILE))
    grad = None
    for k in range(3):
        for l in range(LAYERS):
            rhs = sloc[k, :, l * PLANE:(l + 1) * PLANE]
            row = res_ref[k:k + 1, l * PLANE:(l + 1) * PLANE].astype(F32)
            lhs = jnp.broadcast_to(row, (16, PLANE)).astype(BF)
            got = lax.dot_general(lhs, rhs, NT, preferred_element_type=F32)
            grad = got if grad is None else grad + got
    row16 = iota((16, TILE), 0)
    pieces = []
    for l in range(LAYERS):
        x = mis_ref[pl.ds(l, 1), ctile]
        hi = x.astype(BF).astype(F32)
        mid = (x - hi).astype(BF).astype(F32)
        lo = x - hi - mid
        full = jnp.where(row16 == 0, jnp.broadcast_to(hi, (16, TILE)), 0.0)
        full = jnp.where(row16 == 1, jnp.broadcast_to(mid, (16, TILE)), full)
        full = jnp.where(row16 == 2, jnp.broadcast_to(lo, (16, TILE)), full)
        pieces.append(full.astype(BF))
    zone_lhs = jnp.concatenate(pieces, axis=1)
    esrc[0] = jnp.zeros((8, TILE), F32)
    esrc[0, 0:1, 0:COLS] = grad[0:1]
    for half in range(2):
        zone_id = iota((256, TILE), 0) + 256 * half
        hot = jnp.concatenate([
            jnp.where(jnp.broadcast_to(lab_ref[pl.ds(l, 1), ctile], (256, TILE)) == zone_id, 1.0, 0.0).astype(BF)
            for l in range(LAYERS)], axis=1)
        got = lax.dot_general(zone_lhs, hot, NT, preferred_element_type=F32)
        got = got[0:1] + got[1:2] + got[2:3]
        esrc[0, 4 + 2 * half:5 + 2 * half, :] = got[:, 0:TILE]
        esrc[0, 5 + 2 * half:6 + 2 * half, :] = got[:, TILE:2 * TILE]

    small0 = pltpu.make_async_remote_copy(
        src_ref=esrc.at[0], dst_ref=e0, send_sem=es.at[0], recv_sem=er.at[0],
        device_id=(partner, c), device_id_type=MESH)

    def small1(i):
        return pltpu.make_async_remote_copy(
            src_ref=esrc.at[1], dst_ref=e1.at[d], send_sem=es.at[1], recv_sem=er.at[1],
            device_id=(slab_peer(*OFFS[i]), c), device_id_type=MESH)

    def small2(i):
        return pltpu.make_async_remote_copy(
            src_ref=esrc.at[2], dst_ref=e2.at[c], send_sem=es.at[2], recv_sem=er.at[2],
            device_id=(s, col_peer(*OFFS[i])), device_id_type=MESH)

    small0.start()

    lane = iota((16, TILE), 1)
    not_first = lax.rem(lane, GY) != 0
    inside = lane >= GY
    edge_lane = iota((32, TILE), 1)

    def block(j):
        src = order[j]
        if j > 0:
            wait_all(chunk.at[src, pl.ds(EDGE + PART, 3 * PART), :], rb.at[src])

        @pl.when(s < 15)
        def _():
            wait_all(above.at[src], fz.at[src])

        for k in range(3):
            low = chunk[src, 32 * k:32 * k + 32, :].astype(F32)
            top = above[src, 32 * k:32 * k + 32, :].astype(F32)
            for h in range(2):
                first = low if h == 0 else pltpu.roll(low, 64, 1)
                second = top if h == 1 else pltpu.roll(top, 64, 1)
                both = jnp.where(edge_lane < 64, first, jnp.where(edge_lane < 80, second, 0.0))
                edges[src, COLS * k + 32 * h:COLS * k + 32 * h + 32, :] = both.astype(BF)
        halo = edges[src]
        for l in range(LAYERS + 1):
            if l < LAYERS:
                here = chunk[src, EDGE + l * PART:EDGE + (l + 1) * PART, :]
            else:
                here = above[src, EDGE:EDGE + PART, :]
            got = jnp.dot(jnp.concatenate([here, halo], axis=1), w_ref[l], preferred_element_type=F32)
            fbuf[l] = got.reshape(3, COLS, 4 * TILE)

        @pl.loop(0, COLS // 16)
        def _(r):
            rows = pl.ds(pl.multiple_of(r * 16, 16), 16)
            dest = pl.ds(pl.multiple_of(src * COLS + r * 16, 16), 16)
            carry = [[None] * 3 for _ in range(4)]
            edge = [jnp.zeros((16, TILE), F32) for _ in range(3)]
            for n in range(LAYERS + 1):
                unit = [[None] * 3 for _ in range(4)]
                if n < LAYERS:
                    g = [gbuf[k, n] for k in range(6)]
                    for q in range(4):
                        low, high = [], []
                        for k in range(3):
                            first = fbuf[n, k, rows, q * TILE:(q + 1) * TILE]
                            second = fbuf[n + 1, k, rows, q * TILE:(q + 1) * TILE]
                            both = first + second
                            low.append(first + both)
                            high.append(second + both)

                        def apply(v):
                            return [
                                g[0] * v[0] + g[3] * v[1] + g[4] * v[2],
                                g[3] * v[0] + g[1] * v[1] + g[5] * v[2],
                                g[4] * v[0] + g[5] * v[1] + g[2] * v[2],
                            ]

                        low, high = apply(low), apply(high)
                        for k in range(3):
                            unit[q][k] = low[k] if n == 0 else carry[q][k] + low[k]
                            carry[q][k] = high[k]
                else:
                    unit = carry
                for k in range(3):
                    near = unit[0][k] + jnp.where(not_first, pltpu.roll(unit[1][k], 1, 1), 0.0)
                    far = unit[2][k] + jnp.where(not_first, pltpu.roll(unit[3][k], 1, 1), 0.0)
                    moved = pltpu.roll(far, GY, 1)
                    img[k, dest, n * TILE:(n + 1) * TILE] = (near + jnp.where(inside, moved, 0.0)).astype(BF)
                    if n > 0:
                        moved = pltpu.roll(far, GY * (n + 1), 1)
                    edge[k] = jnp.where((lane >= GY * n) & (lane < GY * (n + 1)), moved, edge[k])
            for k in range(3):
                img[k, dest, KW - TILE:KW] = edge[k].astype(BF)

    wait_all(chunk.at[pl.ds(0, 7), pl.ds(0, EDGE + PART), :], sa)
    groups = ((0, 1, 2), (3,), (4,), (5,), (6,))

    def send_group(g):
        for i in groups[g]:
            for l in range(1, LAYERS):
                send(i, l, sb.at[g], rb)

    def group_left(g):
        wait_all(chunk.at[pl.ds(0, len(groups[g])), pl.ds(EDGE + PART, 3 * PART), :], sb.at[g])

    send_group(0)
    send_group(1)
    send_group(2)
    for j in range(1, 4):
        arrive(j)
    block(0)
    group_left(0)
    send_group(3)
    small0.wait_recv()
    esrc[1] = esrc[0] + e0[...]
    for i in range(7):
        small1(i).start()
    e1[d] = esrc[1]
    for j in range(4, 8):
        arrive(j)
    for j in range(1, 8):
        if j == 3:
            group_left(1)
            send_group(4)
        block(j)
        if j == 4:
            wait_all(e1.at[pl.ds(0, 7)], er.at[1])
            total = e1[0]
            for who in range(1, 8):
                total = total + e1[who]
            esrc[2] = total
            for i in range(7):
                small2(i).start()
            e2[c] = total

    def panel(half):
        total = None
        for k in range(3):
            rhs = []
            for e in range(8):
                rows = pl.ds(pl.multiple_of(EDGE + k * COLS + half * 32, 32), 32)
                tiles = [
                    chunk[e, pl.ds(pl.multiple_of(EDGE + l * PART + k * COLS + half * 32, 32), 32), :]
                    for l in range(LAYERS)]
                tiles.append(above[e, rows, :])
                tiles.append(edges[e, pl.ds(pl.multiple_of(k * COLS + half * 32, 32), 32), :])
                rhs.append(jnp.concatenate(tiles, axis=1))
            got = lax.dot_general(img[k], jnp.concatenate(rhs, axis=0), NT, preferred_element_type=F32)
            total = got if total is None else total + got
        hacc[half] = total

    other = 1 - core
    panel(other)
    def swap(i):
        rows = pl.ds(pl.multiple_of(lax.rem(c + i, 8) * COLS, COLS), COLS)
        return pltpu.make_async_remote_copy(
            src_ref=hacc.at[other, rows, :], dst_ref=hrecv.at[rows, :], send_sem=p0_sem.at[i], recv_sem=p1_sem.at[i],
            device_id=(partner, c), device_id_type=MESH)

    for i in range(8):
        swap(i).start()
    panel(core)

    wait_all(e2.at[pl.ds(0, 7)], er.at[2])

    me = c * 8 + d
    group = lane // 32
    for i in range(8):
        to_c = lax.rem(c + i, 8)
        swap(i).wait_recv()
        sums = []
        for g in range(4):
            rows = pl.ds(pl.multiple_of(to_c * COLS + 16 * g, 16), 16)
            sums.append(hacc[core, rows, :] + hrecv[rows, :])
        for e in range(8):
            a, b = e // 4, e % 4
            packed = None
            for g in range(4):
                piece = sums[g][:, a * TILE:(a + 1) * TILE]
                shift = (32 * g - 32 * b) % TILE
                if shift:
                    piece = pltpu.roll(piece, shift, 1)
                packed = piece if packed is None else jnp.where(group == g, piece, packed)
            pack[to_c * 8 + e] = packed
        for j in range(8):
            if i + j == 0:
                continue
            to_d = lax.rem(d + j, 8)
            pltpu.make_async_remote_copy(
                src_ref=pack.at[to_c * 8 + to_d], dst_ref=parts.at[me], send_sem=msem, recv_sem=rsem,
                device_id=(to_d * 2 + core, to_c), device_id_type=MESH).start()
    parts[me] = pack[me]

    zone = e2[0]
    for who in range(1, 8):
        zone = zone + e2[who]
    out_ref[36:40, :] = zone[4:8] * (WIDTH / 65536)
    left = iota((1, TILE), 1) < COLS
    for t in range(4):
        out_ref[32 + t:33 + t, :] = jnp.where(left, e2[2 * t, 0:1, :], pltpu.roll(e2[2 * t + 1, 0:1, :], COLS, 1))

    wait_all(parts.at[pl.ds(0, 63)], rsem)
    total = parts[0]
    for who in range(1, 64):
        total = total + parts[who]
    rows = [pltpu.roll(total, TILE - 32 * g, 1) if g else total for g in range(4)]
    out_ref[0:32, 0:COLS] = jnp.transpose(jnp.concatenate(rows, axis=0))[0:32, :]

    @pl.when(s > 0)
    def _():
        for j in range(8):
            forward(j).wait_send()

    group_left(2)
    group_left(3)
    group_left(4)
    small0.wait_send()
    wait_all(e1.at[pl.ds(0, 7)], es.at[1])
    wait_all(e2.at[pl.ds(0, 7)], es.at[2])
    for i in range(8):
        swap(i).wait_send()
    wait_all(parts.at[pl.ds(0, 63)], msem)


def on_device(sensitivity, residual_force, moments, zone_label, misfit):
    any_spec = pl.BlockSpec(memory_space=pl.ANY)
    vmem = pl.BlockSpec(memory_space=pltpu.VMEM)
    dma = pltpu.SemaphoreType.DMA
    out = pl.pallas_call(
        kernel,
        name="gauss_newton",
        out_shape=jax.ShapeDtypeStruct((40, TILE), F32),
        in_specs=[any_spec] * 5,
        out_specs=vmem,
        scratch_shapes=[
            pltpu.VMEM((LAYERS + 1, 2 * TILE, 4 * TILE), BF),
            pltpu.VMEM((2 * LAYERS * TILE, TILE), BF),
            pltpu.VMEM((3, LAYERS * PLANE), BF),
            pltpu.VMEM((6, LAYERS, PLANE), F32),
            pltpu.VMEM((LAYERS, PLANE), jnp.int32),
            pltpu.VMEM((LAYERS, PLANE), F32),
            pltpu.VMEM((3, COLS, LAYERS * PLANE), BF),
            pltpu.VMEM((8, EDGE, TILE), BF),
            pltpu.VMEM((8, CHUNK, TILE), BF),
            pltpu.VMEM((8, EDGE + PART, TILE), BF),
            pltpu.VMEM((8, PART, TILE), BF),
            pltpu.VMEM((3, WIDTH, KW), BF),
            pltpu.VMEM((LAYERS + 1, 3, COLS, 4 * TILE), F32),
            pltpu.VMEM((6, LAYERS, 16, TILE), F32),
            pltpu.VMEM((2, WIDTH, 256), F32),
            pltpu.VMEM((WIDTH, 256), F32),
            pltpu.VMEM((64, 16, TILE), F32),
            pltpu.VMEM((64, 16, TILE), F32),
            pltpu.VMEM((3, 8, TILE), F32),
            pltpu.VMEM((8, TILE), F32),
            pltpu.VMEM((8, 8, TILE), F32),
            pltpu.VMEM((8, 8, TILE), F32),
            dma((4,)), dma((2,)), dma(()), dma((5,)), dma((8,)), dma((8,)), dma((8,)), dma((8,)), dma((8,)), dma((8,)),
            dma((3,)), dma((3,)), dma(()), dma(()),
        ],
        compiler_params=pltpu.CompilerParams(collective_id=0, has_side_effects=True, vmem_limit_bytes=67043328),
    )(sensitivity, residual_force, moments, zone_label, misfit)
    return out[0:32, 0:COLS].T, out[32:36].reshape(WIDTH), out[36:40].reshape(WIDTH)


def solution(mesh):
    in_specs = (
        P(None, "col", "slab"),
        P(None, "slab"),
        P(None, "slab", None),
        P("slab", None),
        P("slab", None),
    )
    out_specs = (P("col", "slab"), P(), P())
    return jax.shard_map(
        on_device, mesh=mesh, in_specs=in_specs, out_specs=out_specs, check_vma=False
    )
```

```python
import jax
import jax.numpy as jnp
from jax import lax
from jax.experimental import pallas as pl
from jax.experimental.pallas import tpu as pltpu
from jax.sharding import PartitionSpec as P

MESH = pl.DeviceIdType.MESH
GX = 64
GY = 16
PLANE = GX * GY
LAYERS = 4
COLS = 64
WIDTH = 512
TILE = 128
KW = 768
EDGE = 3 * 32
PART = 3 * COLS
CHUNK = EDGE + LAYERS * PART
BF = jnp.bfloat16
F32 = jnp.float32
NT = (((1,), (1,)), ((), ()))
FAR = ((1, 2), (1, 1), (1, 3), (0, 2), (1, 0), (0, 1), (0, 3), (0, 0))
OFFS = ((0, 1), (0, 3), (1, 0), (0, 2), (1, 1), (1, 3), (1, 2))


def iota(shape, dim):
    return lax.broadcasted_iota(jnp.int32, shape, dim)


def pair_weight(shift, side):
    return jnp.where(shift == side, 2.0, jnp.where(shift == 1 - side, 1.0, 0.0))


def fill_pick(pick_ref):
    src, dst = iota((TILE, TILE), 0), iota((TILE, TILE), 1)
    for h in range(2):
        for l in range(LAYERS):
            hit = (src == dst - 64 * h - GY * l) & (src < GY)
            at = (h * LAYERS + l) * TILE
            pick_ref[at:at + TILE, :] = jnp.where(hit, 1.0, 0.0).astype(BF)


def fill_weights(w_ref):
    src, elem = iota((TILE, TILE), 0), iota((TILE, TILE), 1)
    ex, ey = elem // GY, lax.rem(elem, GY)
    sx, sy = src // GY, lax.rem(src, GY)
    for b in range(2):
        for c in range(2):
            wy = pair_weight(sy - ey, c)
            at = (2 * b + c) * TILE
            near = (pair_weight(sx - ex, b) * wy).astype(BF)
            far = pair_weight(8 - ex, b) * wy
            for l in range(LAYERS + 1):
                w_ref[l, 0:TILE, at:at + TILE] = near
                w_ref[l, TILE:2 * TILE, at:at + TILE] = jnp.where(sx == l, far, 0.0).astype(BF)


def kernel(
    s_any, res_any, mom_any, lab_any, mis_any,
    out_ref,
    w_ref, pick_ref, res_ref, mom_ref, lab_ref, mis_ref,
    sloc, hal, chunk, above, edges, img, fbuf, gbuf, hacc, hrecv, pack, parts,
    esrc, e0, e1, e2,
    in_sem, own_sem, sa, sb, ra, rb, fs, fz, p0_sem, p1_sem, es, er, msem, rsem,
):
    s = lax.axis_index("slab")
    c = lax.axis_index("col")
    core = lax.rem(s, 2)
    z = lax.rem(s // 2, 4)
    xh = s // 8
    xl = c // 4
    y = lax.rem(c, 4)
    d = s // 2

    def col_peer(dx, dy):
        return lax.rem(xl + dx, 2) * 4 + lax.rem(y + dy + 4, 4)

    def slab_peer(dx, dz):
        return (lax.rem(xh + dx, 2) * 4 + lax.rem(z + dz + 4, 4)) * 2 + core

    order = [c] + [col_peer(dx, -dy) for dx, dy in OFFS]
    partner = s + 1 - 2 * core
    below = lax.rem(s + 15, 16)
    bar = pltpu.get_barrier_semaphore()
    for dx, dy in OFFS:
        pl.semaphore_signal(bar, inc=1, device_id=(s, col_peer(dx, dy)), device_id_type=MESH)
        pl.semaphore_signal(bar, inc=1, device_id=(slab_peer(dx, dy), c), device_id_type=MESH)
    for to in (partner, lax.rem(s + 1, 16), below):
        pl.semaphore_signal(bar, inc=1, device_id=(to, c), device_id_type=MESH)

    def wait_all(ref, sem):
        pltpu.make_async_copy(ref, ref, sem).wait()

    def lanes(l, who):
        return pl.ds(pl.multiple_of(l * PLANE + who * TILE, TILE), TILE)

    def tile_rows(l, k):
        return pl.ds(EDGE + l * PART + k * COLS, COLS)

    whole = pltpu.make_async_copy(s_any, sloc, own_sem.at[0])
    whole.start()
    for l in range(LAYERS):
        for k in range(3):
            pltpu.make_async_copy(
                s_any.at[k, :, lanes(l, c)], chunk.at[c, tile_rows(l, k), :], own_sem.at[1]).start()
    loads = [
        pltpu.make_async_copy(a, b, in_sem.at[i])
        for i, (a, b) in enumerate(((res_any, res_ref), (mom_any, mom_ref), (lab_any, lab_ref), (mis_any, mis_ref)))]
    for load in loads:
        load.start()

    @pl.when(s == 15)
    def _():
        above[...] = jnp.zeros_like(above)

    pl.semaphore_wait(bar, 17)

    def send(i, l, sem, to):
        who = col_peer(*OFFS[i])
        for k in range(3):
            pltpu.make_async_remote_copy(
                src_ref=s_any.at[k, :, lanes(l, who)], dst_ref=chunk.at[c, tile_rows(l, k), :],
                send_sem=sem, recv_sem=to.at[c], device_id=(s, who), device_id_type=MESH).start()

    for i in range(7):
        send(i, 0, sa, ra)
    fill_pick(pick_ref)
    whole.wait()
    for who in range(8):
        if who == 7:
            hal[7] = jnp.zeros((EDGE, TILE), BF)
        else:
            tiles = []
            for h in range(2):
                for l in range(LAYERS):
                    at = l * PLANE + (who + 1) * TILE
                    tiles.append(jnp.concatenate(
                        [sloc[k, 32 * h:32 * h + 32, at:at + TILE] for k in range(3)], axis=0))
            got = jnp.dot(jnp.concatenate(tiles, axis=1), pick_ref[...], preferred_element_type=F32)
            hal[who] = got.astype(BF)
    for i in range(7):
        who = col_peer(*OFFS[i])
        pltpu.make_async_remote_copy(
            src_ref=hal.at[who], dst_ref=chunk.at[c, pl.ds(0, EDGE), :],
            send_sem=sa, recv_sem=ra.at[c], device_id=(s, who), device_id_type=MESH).start()
    chunk[c, 0:EDGE, :] = hal[c]
    wait_all(chunk.at[c, pl.ds(EDGE, LAYERS * PART), :], own_sem.at[1])

    def forward(j):
        src = order[j]
        return pltpu.make_async_remote_copy(
            src_ref=chunk.at[src, pl.ds(0, EDGE + PART), :], dst_ref=above.at[src],
            send_sem=fs.at[j], recv_sem=fz.at[src], device_id=(below, c), device_id_type=MESH)

    def arrive(j):
        src = order[j]
        if j > 0:
            wait_all(chunk.at[src, pl.ds(0, EDGE + PART), :], ra.at[src])

        @pl.when(s > 0)
        def _():
            forward(j).start()

    arrive(0)
    fill_weights(w_ref)
    for load in loads:
        load.wait()
    ctile = pl.ds(pl.multiple_of(c * TILE, TILE), TILE)
    for k in range(6):
        for l in range(LAYERS):
            gbuf[k, l] = jnp.broadcast_to(mom_ref[k, pl.ds(l, 1), ctile] * (1.0 / 216.0), (16, TILE))
    grad = None
    for k in range(3):
        for l in range(LAYERS):
            rhs = sloc[k, :, l * PLANE:(l + 1) * PLANE]
            row = res_ref[k:k + 1, l * PLANE:(l + 1) * PLANE].astype(F32)
            lhs = jnp.broadcast_to(row, (16, PLANE)).astype(BF)
            got = lax.dot_general(lhs, rhs, NT, preferred_element_type=F32)
            grad = got if grad is None else grad + got
    row16 = iota((16, TILE), 0)
    pieces = []
    for l in range(LAYERS):
        x = mis_ref[pl.ds(l, 1), ctile]
        hi = x.astype(BF).astype(F32)
        mid = (x - hi).astype(BF).astype(F32)
        lo = x - hi - mid
        full = jnp.where(row16 == 0, jnp.broadcast_to(hi, (16, TILE)), 0.0)
        full = jnp.where(row16 == 1, jnp.broadcast_to(mid, (16, TILE)), full)
        full = jnp.where(row16 == 2, jnp.broadcast_to(lo, (16, TILE)), full)
        pieces.append(full.astype(BF))
    zone_lhs = jnp.concatenate(pieces, axis=1)
    esrc[0] = jnp.zeros((8, TILE), F32)
    esrc[0, 0:1, 0:COLS] = grad[0:1]
    for half in range(2):
        zone_id = iota((256, TILE), 0) + 256 * half
        hot = jnp.concatenate([
            jnp.where(jnp.broadcast_to(lab_ref[pl.ds(l, 1), ctile], (256, TILE)) == zone_id, 1.0, 0.0).astype(BF)
            for l in range(LAYERS)], axis=1)
        got = lax.dot_general(zone_lhs, hot, NT, preferred_element_type=F32)
        got = got[0:1] + got[1:2] + got[2:3]
        esrc[0, 4 + 2 * half:5 + 2 * half, :] = got[:, 0:TILE]
        esrc[0, 5 + 2 * half:6 + 2 * half, :] = got[:, TILE:2 * TILE]

    small0 = pltpu.make_async_remote_copy(
        src_ref=esrc.at[0], dst_ref=e0, send_sem=es.at[0], recv_sem=er.at[0],
        device_id=(partner, c), device_id_type=MESH)

    def small1(i):
        return pltpu.make_async_remote_copy(
            src_ref=esrc.at[1], dst_ref=e1.at[d], send_sem=es.at[1], recv_sem=er.at[1],
            device_id=(slab_peer(*OFFS[i]), c), device_id_type=MESH)

    def small2(i):
        return pltpu.make_async_remote_copy(
            src_ref=esrc.at[2], dst_ref=e2.at[c], send_sem=es.at[2], recv_sem=er.at[2],
            device_id=(s, col_peer(*OFFS[i])), device_id_type=MESH)

    small0.start()

    lane = iota((16, TILE), 1)
    not_first = lax.rem(lane, GY) != 0
    inside = lane >= GY
    edge_lane = iota((32, TILE), 1)

    def block(j):
        src = order[j]
        if j > 0:
            wait_all(chunk.at[src, pl.ds(EDGE + PART, 3 * PART), :], rb.at[src])

        @pl.when(s < 15)
        def _():
            wait_all(above.at[src], fz.at[src])

        for k in range(3):
            low = chunk[src, 32 * k:32 * k + 32, :].astype(F32)
            top = above[src, 32 * k:32 * k + 32, :].astype(F32)
            for h in range(2):
                first = low if h == 0 else pltpu.roll(low, 64, 1)
                second = top if h == 1 else pltpu.roll(top, 64, 1)
                both = jnp.where(edge_lane < 64, first, jnp.where(edge_lane < 80, second, 0.0))
                edges[src, COLS * k + 32 * h:COLS * k + 32 * h + 32, :] = both.astype(BF)
        halo = edges[src]
        for l in range(LAYERS + 1):
            if l < LAYERS:
                here = chunk[src, EDGE + l * PART:EDGE + (l + 1) * PART, :]
            else:
                here = above[src, EDGE:EDGE + PART, :]
            got = jnp.dot(jnp.concatenate([here, halo], axis=1), w_ref[l], preferred_element_type=F32)
            fbuf[l] = got.reshape(3, COLS, 4 * TILE)

        @pl.loop(0, COLS // 16)
        def _(r):
            rows = pl.ds(pl.multiple_of(r * 16, 16), 16)
            dest = pl.ds(pl.multiple_of(src * COLS + r * 16, 16), 16)
            carry = [[None] * 3 for _ in range(4)]
            edge = [jnp.zeros((16, TILE), F32) for _ in range(3)]
            for n in range(LAYERS + 1):
                unit = [[None] * 3 for _ in range(4)]
                if n < LAYERS:
                    g = [gbuf[k, n] for k in range(6)]
                    for q in range(4):
                        low, high = [], []
                        for k in range(3):
                            first = fbuf[n, k, rows, q * TILE:(q + 1) * TILE]
                            second = fbuf[n + 1, k, rows, q * TILE:(q + 1) * TILE]
                            both = first + second
                            low.append(first + both)
                            high.append(second + both)

                        def apply(v):
                            return [
                                g[0] * v[0] + g[3] * v[1] + g[4] * v[2],
                                g[3] * v[0] + g[1] * v[1] + g[5] * v[2],
                                g[4] * v[0] + g[5] * v[1] + g[2] * v[2],
                            ]

                        low, high = apply(low), apply(high)
                        for k in range(3):
                            unit[q][k] = low[k] if n == 0 else carry[q][k] + low[k]
                            carry[q][k] = high[k]
                else:
                    unit = carry
                for k in range(3):
                    near = unit[0][k] + jnp.where(not_first, pltpu.roll(unit[1][k], 1, 1), 0.0)
                    far = unit[2][k] + jnp.where(not_first, pltpu.roll(unit[3][k], 1, 1), 0.0)
                    moved = pltpu.roll(far, GY, 1)
                    img[k, dest, n * TILE:(n + 1) * TILE] = (near + jnp.where(inside, moved, 0.0)).astype(BF)
                    if n > 0:
                        moved = pltpu.roll(far, GY * (n + 1), 1)
                    edge[k] = jnp.where((lane >= GY * n) & (lane < GY * (n + 1)), moved, edge[k])
            for k in range(3):
                img[k, dest, KW - TILE:KW] = edge[k].astype(BF)

    wait_all(chunk.at[pl.ds(0, 7), pl.ds(0, EDGE + PART), :], sa)
    groups = ((0, 1, 2), (3,), (4,), (5,), (6,))

    def send_group(g):
        for i in groups[g]:
            for l in range(1, LAYERS):
                send(i, l, sb.at[g], rb)

    def group_left(g):
        wait_all(chunk.at[pl.ds(0, len(groups[g])), pl.ds(EDGE + PART, 3 * PART), :], sb.at[g])

    send_group(0)
    send_group(1)
    send_group(2)
    for j in range(1, 4):
        arrive(j)
    block(0)
    group_left(0)
    send_group(3)
    small0.wait_recv()
    esrc[1] = esrc[0] + e0[...]
    for i in range(7):
        small1(i).start()
    e1[d] = esrc[1]
    for j in range(4, 8):
        arrive(j)
    for j in range(1, 8):
        if j == 3:
            group_left(1)
            send_group(4)
        block(j)
        if j == 4:
            wait_all(e1.at[pl.ds(0, 7)], er.at[1])
            total = e1[0]
            for who in range(1, 8):
                total = total + e1[who]
            esrc[2] = total
            for i in range(7):
                small2(i).start()
            e2[c] = total

    def panel(half):
        total = None
        for k in range(3):
            rhs = []
            for e in range(8):
                rows = pl.ds(pl.multiple_of(EDGE + k * COLS + half * 32, 32), 32)
                tiles = [
                    chunk[e, pl.ds(pl.multiple_of(EDGE + l * PART + k * COLS + half * 32, 32), 32), :]
                    for l in range(LAYERS)]
                tiles.append(above[e, rows, :])
                tiles.append(edges[e, pl.ds(pl.multiple_of(k * COLS + half * 32, 32), 32), :])
                rhs.append(jnp.concatenate(tiles, axis=1))
            got = lax.dot_general(img[k], jnp.concatenate(rhs, axis=0), NT, preferred_element_type=F32)
            total = got if total is None else total + got
        hacc[half] = total

    other = 1 - core
    panel(other)
    def swap(i):
        rows = pl.ds(pl.multiple_of(col_peer(*FAR[i]) * COLS, COLS), COLS)
        return pltpu.make_async_remote_copy(
            src_ref=hacc.at[other, rows, :], dst_ref=hrecv.at[rows, :], send_sem=p0_sem.at[i], recv_sem=p1_sem.at[i],
            device_id=(partner, c), device_id_type=MESH)

    for i in range(8):
        swap(i).start()
    panel(core)

    wait_all(e2.at[pl.ds(0, 7)], er.at[2])

    me = c * 8 + d
    group = lane // 32
    for i in range(8):
        to_c = col_peer(*FAR[i])
        swap(i).wait_recv()
        sums = []
        for g in range(4):
            rows = pl.ds(pl.multiple_of(to_c * COLS + 16 * g, 16), 16)
            sums.append(hacc[core, rows, :] + hrecv[rows, :])
        for e in range(8):
            a, b = e // 4, e % 4
            packed = None
            for g in range(4):
                piece = sums[g][:, a * TILE:(a + 1) * TILE]
                shift = (32 * g - 32 * b) % TILE
                if shift:
                    piece = pltpu.roll(piece, shift, 1)
                packed = piece if packed is None else jnp.where(group == g, piece, packed)
            pack[to_c * 8 + e] = packed
        for j in range(8):
            if i + j == 14:
                continue
            to_d = slab_peer(*FAR[j]) // 2
            pltpu.make_async_remote_copy(
                src_ref=pack.at[to_c * 8 + to_d], dst_ref=parts.at[me], send_sem=msem, recv_sem=rsem,
                device_id=(to_d * 2 + core, to_c), device_id_type=MESH).start()
    parts[me] = pack[me]

    zone = e2[0]
    for who in range(1, 8):
        zone = zone + e2[who]
    out_ref[36:40, :] = zone[4:8] * (WIDTH / 65536)
    left = iota((1, TILE), 1) < COLS
    for t in range(4):
        out_ref[32 + t:33 + t, :] = jnp.where(left, e2[2 * t, 0:1, :], pltpu.roll(e2[2 * t + 1, 0:1, :], COLS, 1))

    wait_all(parts.at[pl.ds(0, 63)], rsem)
    total = parts[0]
    for who in range(1, 64):
        total = total + parts[who]
    rows = [pltpu.roll(total, TILE - 32 * g, 1) if g else total for g in range(4)]
    out_ref[0:32, 0:COLS] = jnp.transpose(jnp.concatenate(rows, axis=0))[0:32, :]

    @pl.when(s > 0)
    def _():
        for j in range(8):
            forward(j).wait_send()

    group_left(2)
    group_left(3)
    group_left(4)
    small0.wait_send()
    wait_all(e1.at[pl.ds(0, 7)], es.at[1])
    wait_all(e2.at[pl.ds(0, 7)], es.at[2])
    for i in range(8):
        swap(i).wait_send()
    wait_all(parts.at[pl.ds(0, 63)], msem)


def on_device(sensitivity, residual_force, moments, zone_label, misfit):
    any_spec = pl.BlockSpec(memory_space=pl.ANY)
    vmem = pl.BlockSpec(memory_space=pltpu.VMEM)
    dma = pltpu.SemaphoreType.DMA
    out = pl.pallas_call(
        kernel,
        name="gauss_newton",
        out_shape=jax.ShapeDtypeStruct((40, TILE), F32),
        in_specs=[any_spec] * 5,
        out_specs=vmem,
        scratch_shapes=[
            pltpu.VMEM((LAYERS + 1, 2 * TILE, 4 * TILE), BF),
            pltpu.VMEM((2 * LAYERS * TILE, TILE), BF),
            pltpu.VMEM((3, LAYERS * PLANE), BF),
            pltpu.VMEM((6, LAYERS, PLANE), F32),
            pltpu.VMEM((LAYERS, PLANE), jnp.int32),
            pltpu.VMEM((LAYERS, PLANE), F32),
            pltpu.VMEM((3, COLS, LAYERS * PLANE), BF),
            pltpu.VMEM((8, EDGE, TILE), BF),
            pltpu.VMEM((8, CHUNK, TILE), BF),
            pltpu.VMEM((8, EDGE + PART, TILE), BF),
            pltpu.VMEM((8, PART, TILE), BF),
            pltpu.VMEM((3, WIDTH, KW), BF),
            pltpu.VMEM((LAYERS + 1, 3, COLS, 4 * TILE), F32),
            pltpu.VMEM((6, LAYERS, 16, TILE), F32),
            pltpu.VMEM((2, WIDTH, 256), F32),
            pltpu.VMEM((WIDTH, 256), F32),
            pltpu.VMEM((64, 16, TILE), F32),
            pltpu.VMEM((64, 16, TILE), F32),
            pltpu.VMEM((3, 8, TILE), F32),
            pltpu.VMEM((8, TILE), F32),
            pltpu.VMEM((8, 8, TILE), F32),
            pltpu.VMEM((8, 8, TILE), F32),
            dma((4,)), dma((2,)), dma(()), dma((5,)), dma((8,)), dma((8,)), dma((8,)), dma((8,)), dma((8,)), dma((8,)),
            dma((3,)), dma((3,)), dma(()), dma(()),
        ],
        compiler_params=pltpu.CompilerParams(collective_id=0, has_side_effects=True, vmem_limit_bytes=67043328),
    )(sensitivity, residual_force, moments, zone_label, misfit)
    return out[0:32, 0:COLS].T, out[32:36].reshape(WIDTH), out[36:40].reshape(WIDTH)


def solution(mesh):
    in_specs = (
        P(None, "col", "slab"),
        P(None, "slab"),
        P(None, "slab", None),
        P("slab", None),
        P("slab", None),
    )
    out_specs = (P("col", "slab"), P(), P())
    return jax.shard_map(
        on_device, mesh=mesh, in_specs=in_specs, out_specs=out_specs, check_vma=False
    )
```

```python
import jax
import jax.numpy as jnp
from jax import lax
from jax.experimental import pallas as pl
from jax.experimental.pallas import tpu as pltpu
from jax.sharding import PartitionSpec as P

MESH = pl.DeviceIdType.MESH
GX = 64
GY = 16
PLANE = GX * GY
LAYERS = 4
COLS = 64
WIDTH = 512
TILE = 128
KW = 768
EDGE = 3 * 32
PART = 3 * COLS
CHUNK = EDGE + LAYERS * PART
BF = jnp.bfloat16
F32 = jnp.float32
NT = (((1,), (1,)), ((), ()))
FAR = ((1, 2), (1, 1), (1, 3), (0, 2), (1, 0), (0, 1), (0, 3), (0, 0))
OFFS = ((0, 1), (0, 3), (1, 0), (0, 2), (1, 1), (1, 3), (1, 2))


def iota(shape, dim):
    return lax.broadcasted_iota(jnp.int32, shape, dim)


def pair_weight(shift, side):
    return jnp.where(shift == side, 2.0, jnp.where(shift == 1 - side, 1.0, 0.0))


def fill_pick(pick_ref):
    src, dst = iota((TILE, TILE), 0), iota((TILE, TILE), 1)
    for h in range(2):
        for l in range(LAYERS):
            hit = (src == dst - 64 * h - GY * l) & (src < GY)
            at = (h * LAYERS + l) * TILE
            pick_ref[at:at + TILE, :] = jnp.where(hit, 1.0, 0.0).astype(BF)


def fill_weights(w_ref):
    src, elem = iota((TILE, TILE), 0), iota((TILE, TILE), 1)
    ex, ey = elem // GY, lax.rem(elem, GY)
    sx, sy = src // GY, lax.rem(src, GY)
    for b in range(2):
        for c in range(2):
            wy = pair_weight(sy - ey, c)
            at = (2 * b + c) * TILE
            near = (pair_weight(sx - ex, b) * wy).astype(BF)
            far = pair_weight(8 - ex, b) * wy
            for l in range(LAYERS + 1):
                w_ref[l, 0:TILE, at:at + TILE] = near
                w_ref[l, TILE:2 * TILE, at:at + TILE] = jnp.where(sx == l, far, 0.0).astype(BF)


def kernel(
    s_any, res_any, mom_any, lab_any, mis_any,
    out_ref,
    w_ref, pick_ref, res_ref, mom_ref, lab_ref, mis_ref,
    sloc, hal, chunk, above, edges, img, fbuf, gbuf, hacc, hrecv, pack, parts,
    esrc, e0, e1, e2,
    in_sem, own_sem, sa, sb, ra, rb, fs, fz, p0_sem, p1_sem, es, er, msem, rsem,
):
    s = lax.axis_index("slab")
    c = lax.axis_index("col")
    core = lax.rem(s, 2)
    z = lax.rem(s // 2, 4)
    xh = s // 8
    xl = c // 4
    y = lax.rem(c, 4)
    d = s // 2

    def col_peer(dx, dy):
        return lax.rem(xl + dx, 2) * 4 + lax.rem(y + dy + 4, 4)

    def slab_peer(dx, dz):
        return (lax.rem(xh + dx, 2) * 4 + lax.rem(z + dz + 4, 4)) * 2 + core

    order = [c] + [col_peer(dx, -dy) for dx, dy in OFFS]
    partner = s + 1 - 2 * core
    below = lax.rem(s + 15, 16)
    bar = pltpu.get_barrier_semaphore()
    for dx, dy in OFFS:
        pl.semaphore_signal(bar, inc=1, device_id=(s, col_peer(dx, dy)), device_id_type=MESH)
        pl.semaphore_signal(bar, inc=1, device_id=(slab_peer(dx, dy), c), device_id_type=MESH)
    for to in (partner, lax.rem(s + 1, 16), below):
        pl.semaphore_signal(bar, inc=1, device_id=(to, c), device_id_type=MESH)

    def wait_all(ref, sem):
        pltpu.make_async_copy(ref, ref, sem).wait()

    def lanes(l, who):
        return pl.ds(pl.multiple_of(l * PLANE + who * TILE, TILE), TILE)

    def tile_rows(l, k):
        return pl.ds(EDGE + l * PART + k * COLS, COLS)

    whole = pltpu.make_async_copy(s_any, sloc, own_sem.at[0])
    whole.start()
    for l in range(LAYERS):
        for k in range(3):
            pltpu.make_async_copy(
                s_any.at[k, :, lanes(l, c)], chunk.at[c, tile_rows(l, k), :], own_sem.at[1]).start()
    loads = [
        pltpu.make_async_copy(a, b, in_sem.at[i])
        for i, (a, b) in enumerate(((res_any, res_ref), (mom_any, mom_ref), (lab_any, lab_ref), (mis_any, mis_ref)))]
    for load in loads:
        load.start()

    @pl.when(s == 15)
    def _():
        above[...] = jnp.zeros_like(above)

    pl.semaphore_wait(bar, 17)

    def send(i, l, sem, to):
        who = col_peer(*OFFS[i])
        for k in range(3):
            pltpu.make_async_remote_copy(
                src_ref=s_any.at[k, :, lanes(l, who)], dst_ref=chunk.at[c, tile_rows(l, k), :],
                send_sem=sem, recv_sem=to.at[c], device_id=(s, who), device_id_type=MESH).start()

    for i in range(7):
        send(i, 0, sa, ra)
    fill_pick(pick_ref)
    whole.wait()
    for who in range(8):
        if who == 7:
            hal[7] = jnp.zeros((EDGE, TILE), BF)
        else:
            tiles = []
            for h in range(2):
                for l in range(LAYERS):
                    at = l * PLANE + (who + 1) * TILE
                    tiles.append(jnp.concatenate(
                        [sloc[k, 32 * h:32 * h + 32, at:at + TILE] for k in range(3)], axis=0))
            got = jnp.dot(jnp.concatenate(tiles, axis=1), pick_ref[...], preferred_element_type=F32)
            hal[who] = got.astype(BF)
    for i in range(7):
        who = col_peer(*OFFS[i])
        pltpu.make_async_remote_copy(
            src_ref=hal.at[who], dst_ref=chunk.at[c, pl.ds(0, EDGE), :],
            send_sem=sa, recv_sem=ra.at[c], device_id=(s, who), device_id_type=MESH).start()
    groups = ((0, 1, 2), (3,), (4,), (5,), (6,))

    def send_group(g):
        for i in groups[g]:
            for l in range(1, LAYERS):
                send(i, l, sb.at[g], rb)

    def group_left(g):
        wait_all(chunk.at[pl.ds(0, len(groups[g])), pl.ds(EDGE + PART, 3 * PART), :], sb.at[g])

    send_group(0)
    chunk[c, 0:EDGE, :] = hal[c]
    wait_all(chunk.at[c, pl.ds(EDGE, LAYERS * PART), :], own_sem.at[1])

    def forward(j):
        src = order[j]
        return pltpu.make_async_remote_copy(
            src_ref=chunk.at[src, pl.ds(0, EDGE + PART), :], dst_ref=above.at[src],
            send_sem=fs.at[j], recv_sem=fz.at[src], device_id=(below, c), device_id_type=MESH)

    def arrive(j):
        src = order[j]
        if j > 0:
            wait_all(chunk.at[src, pl.ds(0, EDGE + PART), :], ra.at[src])

        @pl.when(s > 0)
        def _():
            forward(j).start()

    arrive(0)
    fill_weights(w_ref)
    for load in loads:
        load.wait()
    ctile = pl.ds(pl.multiple_of(c * TILE, TILE), TILE)
    for k in range(6):
        for l in range(LAYERS):
            gbuf[k, l] = jnp.broadcast_to(mom_ref[k, pl.ds(l, 1), ctile] * (1.0 / 216.0), (16, TILE))
    grad = None
    for k in range(3):
        for l in range(LAYERS):
            rhs = sloc[k, :, l * PLANE:(l + 1) * PLANE]
            row = res_ref[k:k + 1, l * PLANE:(l + 1) * PLANE].astype(F32)
            lhs = jnp.broadcast_to(row, (16, PLANE)).astype(BF)
            got = lax.dot_general(lhs, rhs, NT, preferred_element_type=F32)
            grad = got if grad is None else grad + got
    row16 = iota((16, TILE), 0)
    pieces = []
    for l in range(LAYERS):
        x = mis_ref[pl.ds(l, 1), ctile]
        hi = x.astype(BF).astype(F32)
        mid = (x - hi).astype(BF).astype(F32)
        lo = x - hi - mid
        full = jnp.where(row16 == 0, jnp.broadcast_to(hi, (16, TILE)), 0.0)
        full = jnp.where(row16 == 1, jnp.broadcast_to(mid, (16, TILE)), full)
        full = jnp.where(row16 == 2, jnp.broadcast_to(lo, (16, TILE)), full)
        pieces.append(full.astype(BF))
    zone_lhs = jnp.concatenate(pieces, axis=1)
    esrc[0] = jnp.zeros((8, TILE), F32)
    esrc[0, 0:1, 0:COLS] = grad[0:1]
    for half in range(2):
        zone_id = iota((256, TILE), 0) + 256 * half
        hot = jnp.concatenate([
            jnp.where(jnp.broadcast_to(lab_ref[pl.ds(l, 1), ctile], (256, TILE)) == zone_id, 1.0, 0.0).astype(BF)
            for l in range(LAYERS)], axis=1)
        got = lax.dot_general(zone_lhs, hot, NT, preferred_element_type=F32)
        got = got[0:1] + got[1:2] + got[2:3]
        esrc[0, 4 + 2 * half:5 + 2 * half, :] = got[:, 0:TILE]
        esrc[0, 5 + 2 * half:6 + 2 * half, :] = got[:, TILE:2 * TILE]

    small0 = pltpu.make_async_remote_copy(
        src_ref=esrc.at[0], dst_ref=e0, send_sem=es.at[0], recv_sem=er.at[0],
        device_id=(partner, c), device_id_type=MESH)

    def small1(i):
        return pltpu.make_async_remote_copy(
            src_ref=esrc.at[1], dst_ref=e1.at[d], send_sem=es.at[1], recv_sem=er.at[1],
            device_id=(slab_peer(*OFFS[i]), c), device_id_type=MESH)

    def small2(i):
        return pltpu.make_async_remote_copy(
            src_ref=esrc.at[2], dst_ref=e2.at[c], send_sem=es.at[2], recv_sem=er.at[2],
            device_id=(s, col_peer(*OFFS[i])), device_id_type=MESH)

    small0.start()

    lane = iota((16, TILE), 1)
    not_first = lax.rem(lane, GY) != 0
    inside = lane >= GY
    edge_lane = iota((32, TILE), 1)

    def block(j):
        src = order[j]
        if j > 0:
            wait_all(chunk.at[src, pl.ds(EDGE + PART, 3 * PART), :], rb.at[src])

        @pl.when(s < 15)
        def _():
            wait_all(above.at[src], fz.at[src])

        for k in range(3):
            low = chunk[src, 32 * k:32 * k + 32, :].astype(F32)
            top = above[src, 32 * k:32 * k + 32, :].astype(F32)
            for h in range(2):
                first = low if h == 0 else pltpu.roll(low, 64, 1)
                second = top if h == 1 else pltpu.roll(top, 64, 1)
                both = jnp.where(edge_lane < 64, first, jnp.where(edge_lane < 80, second, 0.0))
                edges[src, COLS * k + 32 * h:COLS * k + 32 * h + 32, :] = both.astype(BF)
        halo = edges[src]
        for l in range(LAYERS + 1):
            if l < LAYERS:
                here = chunk[src, EDGE + l * PART:EDGE + (l + 1) * PART, :]
            else:
                here = above[src, EDGE:EDGE + PART, :]
            got = jnp.dot(jnp.concatenate([here, halo], axis=1), w_ref[l], preferred_element_type=F32)
            fbuf[l] = got.reshape(3, COLS, 4 * TILE)

        @pl.loop(0, COLS // 16)
        def _(r):
            rows = pl.ds(pl.multiple_of(r * 16, 16), 16)
            dest = pl.ds(pl.multiple_of(src * COLS + r * 16, 16), 16)
            carry = [[None] * 3 for _ in range(4)]
            edge = [jnp.zeros((16, TILE), F32) for _ in range(3)]
            for n in range(LAYERS + 1):
                unit = [[None] * 3 for _ in range(4)]
                if n < LAYERS:
                    g = [gbuf[k, n] for k in range(6)]
                    for q in range(4):
                        low, high = [], []
                        for k in range(3):
                            first = fbuf[n, k, rows, q * TILE:(q + 1) * TILE]
                            second = fbuf[n + 1, k, rows, q * TILE:(q + 1) * TILE]
                            both = first + second
                            low.append(first + both)
                            high.append(second + both)

                        def apply(v):
                            return [
                                g[0] * v[0] + g[3] * v[1] + g[4] * v[2],
                                g[3] * v[0] + g[1] * v[1] + g[5] * v[2],
                                g[4] * v[0] + g[5] * v[1] + g[2] * v[2],
                            ]

                        low, high = apply(low), apply(high)
                        for k in range(3):
                            unit[q][k] = low[k] if n == 0 else carry[q][k] + low[k]
                            carry[q][k] = high[k]
                else:
                    unit = carry
                for k in range(3):
                    near = unit[0][k] + jnp.where(not_first, pltpu.roll(unit[1][k], 1, 1), 0.0)
                    far = unit[2][k] + jnp.where(not_first, pltpu.roll(unit[3][k], 1, 1), 0.0)
                    moved = pltpu.roll(far, GY, 1)
                    img[k, dest, n * TILE:(n + 1) * TILE] = (near + jnp.where(inside, moved, 0.0)).astype(BF)
                    if n > 0:
                        moved = pltpu.roll(far, GY * (n + 1), 1)
                    edge[k] = jnp.where((lane >= GY * n) & (lane < GY * (n + 1)), moved, edge[k])
            for k in range(3):
                img[k, dest, KW - TILE:KW] = edge[k].astype(BF)

    wait_all(chunk.at[pl.ds(0, 7), pl.ds(0, EDGE + PART), :], sa)
    send_group(1)
    send_group(2)
    for j in range(1, 4):
        arrive(j)
    block(0)
    group_left(0)
    send_group(3)
    small0.wait_recv()
    esrc[1] = esrc[0] + e0[...]
    for i in range(7):
        small1(i).start()
    e1[d] = esrc[1]
    for j in range(4, 8):
        arrive(j)
    for j in range(1, 8):
        if j == 3:
            group_left(1)
            send_group(4)
        block(j)
        if j == 4:
            wait_all(e1.at[pl.ds(0, 7)], er.at[1])
            total = e1[0]
            for who in range(1, 8):
                total = total + e1[who]
            esrc[2] = total
            for i in range(7):
                small2(i).start()
            e2[c] = total

    def panel(half):
        total = None
        for k in range(3):
            rhs = []
            for e in range(8):
                rows = pl.ds(pl.multiple_of(EDGE + k * COLS + half * 32, 32), 32)
                tiles = [
                    chunk[e, pl.ds(pl.multiple_of(EDGE + l * PART + k * COLS + half * 32, 32), 32), :]
                    for l in range(LAYERS)]
                tiles.append(above[e, rows, :])
                tiles.append(edges[e, pl.ds(pl.multiple_of(k * COLS + half * 32, 32), 32), :])
                rhs.append(jnp.concatenate(tiles, axis=1))
            got = lax.dot_general(img[k], jnp.concatenate(rhs, axis=0), NT, preferred_element_type=F32)
            total = got if total is None else total + got
        hacc[half] = total

    other = 1 - core
    panel(other)
    def swap(i):
        rows = pl.ds(pl.multiple_of(col_peer(*FAR[i]) * COLS, COLS), COLS)
        return pltpu.make_async_remote_copy(
            src_ref=hacc.at[other, rows, :], dst_ref=hrecv.at[rows, :], send_sem=p0_sem.at[i], recv_sem=p1_sem.at[i],
            device_id=(partner, c), device_id_type=MESH)

    for i in range(8):
        swap(i).start()
    panel(core)

    wait_all(e2.at[pl.ds(0, 7)], er.at[2])

    me = c * 8 + d
    group = lane // 32
    for i in range(8):
        to_c = col_peer(*FAR[i])
        swap(i).wait_recv()
        sums = []
        for g in range(4):
            rows = pl.ds(pl.multiple_of(to_c * COLS + 16 * g, 16), 16)
            sums.append(hacc[core, rows, :] + hrecv[rows, :])
        for e in range(8):
            a, b = e // 4, e % 4
            packed = None
            for g in range(4):
                piece = sums[g][:, a * TILE:(a + 1) * TILE]
                shift = (32 * g - 32 * b) % TILE
                if shift:
                    piece = pltpu.roll(piece, shift, 1)
                packed = piece if packed is None else jnp.where(group == g, piece, packed)
            pack[to_c * 8 + e] = packed
        for j in range(8):
            if i + j == 14:
                continue
            to_d = slab_peer(*FAR[j]) // 2
            pltpu.make_async_remote_copy(
                src_ref=pack.at[to_c * 8 + to_d], dst_ref=parts.at[me], send_sem=msem, recv_sem=rsem,
                device_id=(to_d * 2 + core, to_c), device_id_type=MESH).start()
    parts[me] = pack[me]

    zone = e2[0]
    for who in range(1, 8):
        zone = zone + e2[who]
    out_ref[36:40, :] = zone[4:8] * (WIDTH / 65536)
    left = iota((1, TILE), 1) < COLS
    for t in range(4):
        out_ref[32 + t:33 + t, :] = jnp.where(left, e2[2 * t, 0:1, :], pltpu.roll(e2[2 * t + 1, 0:1, :], COLS, 1))

    wait_all(parts.at[pl.ds(0, 63)], rsem)
    total = parts[0]
    for who in range(1, 64):
        total = total + parts[who]
    rows = [pltpu.roll(total, TILE - 32 * g, 1) if g else total for g in range(4)]
    out_ref[0:32, 0:COLS] = jnp.transpose(jnp.concatenate(rows, axis=0))[0:32, :]

    @pl.when(s > 0)
    def _():
        for j in range(8):
            forward(j).wait_send()

    group_left(2)
    group_left(3)
    group_left(4)
    small0.wait_send()
    wait_all(e1.at[pl.ds(0, 7)], es.at[1])
    wait_all(e2.at[pl.ds(0, 7)], es.at[2])
    for i in range(8):
        swap(i).wait_send()
    wait_all(parts.at[pl.ds(0, 63)], msem)


def on_device(sensitivity, residual_force, moments, zone_label, misfit):
    any_spec = pl.BlockSpec(memory_space=pl.ANY)
    vmem = pl.BlockSpec(memory_space=pltpu.VMEM)
    dma = pltpu.SemaphoreType.DMA
    out = pl.pallas_call(
        kernel,
        name="gauss_newton",
        out_shape=jax.ShapeDtypeStruct((40, TILE), F32),
        in_specs=[any_spec] * 5,
        out_specs=vmem,
        scratch_shapes=[
            pltpu.VMEM((LAYERS + 1, 2 * TILE, 4 * TILE), BF),
            pltpu.VMEM((2 * LAYERS * TILE, TILE), BF),
            pltpu.VMEM((3, LAYERS * PLANE), BF),
            pltpu.VMEM((6, LAYERS, PLANE), F32),
            pltpu.VMEM((LAYERS, PLANE), jnp.int32),
            pltpu.VMEM((LAYERS, PLANE), F32),
            pltpu.VMEM((3, COLS, LAYERS * PLANE), BF),
            pltpu.VMEM((8, EDGE, TILE), BF),
            pltpu.VMEM((8, CHUNK, TILE), BF),
            pltpu.VMEM((8, EDGE + PART, TILE), BF),
            pltpu.VMEM((8, PART, TILE), BF),
            pltpu.VMEM((3, WIDTH, KW), BF),
            pltpu.VMEM((LAYERS + 1, 3, COLS, 4 * TILE), F32),
            pltpu.VMEM((6, LAYERS, 16, TILE), F32),
            pltpu.VMEM((2, WIDTH, 256), F32),
            pltpu.VMEM((WIDTH, 256), F32),
            pltpu.VMEM((64, 16, TILE), F32),
            pltpu.VMEM((64, 16, TILE), F32),
            pltpu.VMEM((3, 8, TILE), F32),
            pltpu.VMEM((8, TILE), F32),
            pltpu.VMEM((8, 8, TILE), F32),
            pltpu.VMEM((8, 8, TILE), F32),
            dma((4,)), dma((2,)), dma(()), dma((5,)), dma((8,)), dma((8,)), dma((8,)), dma((8,)), dma((8,)), dma((8,)),
            dma((3,)), dma((3,)), dma(()), dma(()),
        ],
        compiler_params=pltpu.CompilerParams(collective_id=0, has_side_effects=True, vmem_limit_bytes=67043328),
    )(sensitivity, residual_force, moments, zone_label, misfit)
    return out[0:32, 0:COLS].T, out[32:36].reshape(WIDTH), out[36:40].reshape(WIDTH)


def solution(mesh):
    in_specs = (
        P(None, "col", "slab"),
        P(None, "slab"),
        P(None, "slab", None),
        P("slab", None),
        P("slab", None),
    )
    out_specs = (P("col", "slab"), P(), P())
    return jax.shard_map(
        on_device, mesh=mesh, in_specs=in_specs, out_specs=out_specs, check_vma=False
    )
```

```python
import jax
import jax.numpy as jnp
from jax import lax
from jax.experimental import pallas as pl
from jax.experimental.pallas import tpu as pltpu
from jax.sharding import PartitionSpec as P

MESH = pl.DeviceIdType.MESH
GX = 64
GY = 16
PLANE = GX * GY
LAYERS = 4
COLS = 64
WIDTH = 512
TILE = 128
KW = 768
EDGE = 3 * 32
PART = 3 * COLS
CHUNK = EDGE + LAYERS * PART
BF = jnp.bfloat16
F32 = jnp.float32
NT = (((1,), (1,)), ((), ()))
FAR = ((1, 2), (1, 1), (1, 3), (0, 2), (1, 0), (0, 1), (0, 3), (0, 0))
OFFS = ((0, 1), (0, 3), (1, 0), (0, 2), (1, 1), (1, 3), (1, 2))


def iota(shape, dim):
    return lax.broadcasted_iota(jnp.int32, shape, dim)


def pair_weight(shift, side):
    return jnp.where(shift == side, 2.0, jnp.where(shift == 1 - side, 1.0, 0.0))


def fill_pick(pick_ref):
    src, dst = iota((TILE, TILE), 0), iota((TILE, TILE), 1)
    for h in range(2):
        for l in range(LAYERS):
            hit = (src == dst - 64 * h - GY * l) & (src < GY)
            at = (h * LAYERS + l) * TILE
            pick_ref[at:at + TILE, :] = jnp.where(hit, 1.0, 0.0).astype(BF)


def fill_weights(w_ref):
    src, elem = iota((TILE, TILE), 0), iota((TILE, TILE), 1)
    ex, ey = elem // GY, lax.rem(elem, GY)
    sx, sy = src // GY, lax.rem(src, GY)
    for b in range(2):
        for c in range(2):
            wy = pair_weight(sy - ey, c)
            at = (2 * b + c) * TILE
            near = (pair_weight(sx - ex, b) * wy).astype(BF)
            far = pair_weight(8 - ex, b) * wy
            for l in range(LAYERS + 1):
                w_ref[l, 0:TILE, at:at + TILE] = near
                w_ref[l, TILE:2 * TILE, at:at + TILE] = jnp.where(sx == l, far, 0.0).astype(BF)


def kernel(
    s_any, res_any, mom_any, lab_any, mis_any,
    out_ref,
    w_ref, pick_ref, res_ref, mom_ref, lab_ref, mis_ref,
    sloc, hal, chunk, above, edges, img, fbuf, gbuf, hacc, hrecv, pack, parts,
    esrc, e0, e1, e2,
    in_sem, own_sem, sa, sb, ra, rb, fs, fz, p0_sem, p1_sem, es, er, msem, rsem,
):
    s = lax.axis_index("slab")
    c = lax.axis_index("col")
    core = lax.rem(s, 2)
    z = lax.rem(s // 2, 4)
    xh = s // 8
    xl = c // 4
    y = lax.rem(c, 4)
    d = s // 2

    def col_peer(dx, dy):
        return lax.rem(xl + dx, 2) * 4 + lax.rem(y + dy + 4, 4)

    def slab_peer(dx, dz):
        return (lax.rem(xh + dx, 2) * 4 + lax.rem(z + dz + 4, 4)) * 2 + core

    order = [c] + [col_peer(dx, -dy) for dx, dy in OFFS]
    partner = s + 1 - 2 * core
    below = lax.rem(s + 15, 16)
    bar = pltpu.get_barrier_semaphore()
    for dx, dy in OFFS:
        pl.semaphore_signal(bar, inc=1, device_id=(s, col_peer(dx, dy)), device_id_type=MESH)
        pl.semaphore_signal(bar, inc=1, device_id=(slab_peer(dx, dy), c), device_id_type=MESH)
    for to in (partner, lax.rem(s + 1, 16), below):
        pl.semaphore_signal(bar, inc=1, device_id=(to, c), device_id_type=MESH)

    def wait_all(ref, sem):
        pltpu.make_async_copy(ref, ref, sem).wait()

    def lanes(l, who):
        return pl.ds(pl.multiple_of(l * PLANE + who * TILE, TILE), TILE)

    def tile_rows(l, k):
        return pl.ds(EDGE + l * PART + k * COLS, COLS)

    whole = pltpu.make_async_copy(s_any, sloc, own_sem.at[0])
    whole.start()
    for l in range(LAYERS):
        for k in range(3):
            pltpu.make_async_copy(
                s_any.at[k, :, lanes(l, c)], chunk.at[c, tile_rows(l, k), :], own_sem.at[1]).start()
    loads = [
        pltpu.make_async_copy(a, b, in_sem.at[i])
        for i, (a, b) in enumerate(((res_any, res_ref), (mom_any, mom_ref), (lab_any, lab_ref), (mis_any, mis_ref)))]
    for load in loads:
        load.start()

    @pl.when(s == 15)
    def _():
        above[...] = jnp.zeros_like(above)

    fill_pick(pick_ref)
    pl.semaphore_wait(bar, 17)

    def send(i, l, sem, to):
        who = col_peer(*OFFS[i])
        for k in range(3):
            pltpu.make_async_remote_copy(
                src_ref=s_any.at[k, :, lanes(l, who)], dst_ref=chunk.at[c, tile_rows(l, k), :],
                send_sem=sem, recv_sem=to.at[c], device_id=(s, who), device_id_type=MESH).start()

    for i in range(7):
        send(i, 0, sa, ra)
    whole.wait()
    for who in range(8):
        if who == 7:
            hal[7] = jnp.zeros((EDGE, TILE), BF)
        else:
            tiles = []
            for h in range(2):
                for l in range(LAYERS):
                    at = l * PLANE + (who + 1) * TILE
                    tiles.append(jnp.concatenate(
                        [sloc[k, 32 * h:32 * h + 32, at:at + TILE] for k in range(3)], axis=0))
            got = jnp.dot(jnp.concatenate(tiles, axis=1), pick_ref[...], preferred_element_type=F32)
            hal[who] = got.astype(BF)
    for i in range(7):
        who = col_peer(*OFFS[i])
        pltpu.make_async_remote_copy(
            src_ref=hal.at[who], dst_ref=chunk.at[c, pl.ds(0, EDGE), :],
            send_sem=sa, recv_sem=ra.at[c], device_id=(s, who), device_id_type=MESH).start()
    chunk[c, 0:EDGE, :] = hal[c]
    wait_all(chunk.at[c, pl.ds(EDGE, LAYERS * PART), :], own_sem.at[1])

    def forward(j):
        src = order[j]
        return pltpu.make_async_remote_copy(
            src_ref=chunk.at[src, pl.ds(0, EDGE + PART), :], dst_ref=above.at[src],
            send_sem=fs.at[j], recv_sem=fz.at[src], device_id=(below, c), device_id_type=MESH)

    def arrive(j):
        src = order[j]
        if j > 0:
            wait_all(chunk.at[src, pl.ds(0, EDGE + PART), :], ra.at[src])

        @pl.when(s > 0)
        def _():
            forward(j).start()

    arrive(0)
    fill_weights(w_ref)
    for load in loads:
        load.wait()
    ctile = pl.ds(pl.multiple_of(c * TILE, TILE), TILE)
    for k in range(6):
        for l in range(LAYERS):
            gbuf[k, l] = jnp.broadcast_to(mom_ref[k, pl.ds(l, 1), ctile] * (1.0 / 216.0), (16, TILE))
    grad = None
    for k in range(3):
        for l in range(LAYERS):
            rhs = sloc[k, :, l * PLANE:(l + 1) * PLANE]
            row = res_ref[k:k + 1, l * PLANE:(l + 1) * PLANE].astype(F32)
            lhs = jnp.broadcast_to(row, (16, PLANE)).astype(BF)
            got = lax.dot_general(lhs, rhs, NT, preferred_element_type=F32)
            grad = got if grad is None else grad + got
    row16 = iota((16, TILE), 0)
    pieces = []
    for l in range(LAYERS):
        x = mis_ref[pl.ds(l, 1), ctile]
        hi = x.astype(BF).astype(F32)
        mid = (x - hi).astype(BF).astype(F32)
        lo = x - hi - mid
        full = jnp.where(row16 == 0, jnp.broadcast_to(hi, (16, TILE)), 0.0)
        full = jnp.where(row16 == 1, jnp.broadcast_to(mid, (16, TILE)), full)
        full = jnp.where(row16 == 2, jnp.broadcast_to(lo, (16, TILE)), full)
        pieces.append(full.astype(BF))
    zone_lhs = jnp.concatenate(pieces, axis=1)
    esrc[0] = jnp.zeros((8, TILE), F32)
    esrc[0, 0:1, 0:COLS] = grad[0:1]
    for half in range(2):
        zone_id = iota((256, TILE), 0) + 256 * half
        hot = jnp.concatenate([
            jnp.where(jnp.broadcast_to(lab_ref[pl.ds(l, 1), ctile], (256, TILE)) == zone_id, 1.0, 0.0).astype(BF)
            for l in range(LAYERS)], axis=1)
        got = lax.dot_general(zone_lhs, hot, NT, preferred_element_type=F32)
        got = got[0:1] + got[1:2] + got[2:3]
        esrc[0, 4 + 2 * half:5 + 2 * half, :] = got[:, 0:TILE]
        esrc[0, 5 + 2 * half:6 + 2 * half, :] = got[:, TILE:2 * TILE]

    small0 = pltpu.make_async_remote_copy(
        src_ref=esrc.at[0], dst_ref=e0, send_sem=es.at[0], recv_sem=er.at[0],
        device_id=(partner, c), device_id_type=MESH)

    def small1(i):
        return pltpu.make_async_remote_copy(
            src_ref=esrc.at[1], dst_ref=e1.at[d], send_sem=es.at[1], recv_sem=er.at[1],
            device_id=(slab_peer(*OFFS[i]), c), device_id_type=MESH)

    def small2(i):
        return pltpu.make_async_remote_copy(
            src_ref=esrc.at[2], dst_ref=e2.at[c], send_sem=es.at[2], recv_sem=er.at[2],
            device_id=(s, col_peer(*OFFS[i])), device_id_type=MESH)

    small0.start()

    lane = iota((16, TILE), 1)
    not_first = lax.rem(lane, GY) != 0
    inside = lane >= GY
    edge_lane = iota((32, TILE), 1)

    def block(j):
        src = order[j]
        if j > 0:
            wait_all(chunk.at[src, pl.ds(EDGE + PART, 3 * PART), :], rb.at[src])

        @pl.when(s < 15)
        def _():
            wait_all(above.at[src], fz.at[src])

        for k in range(3):
            low = chunk[src, 32 * k:32 * k + 32, :].astype(F32)
            top = above[src, 32 * k:32 * k + 32, :].astype(F32)
            for h in range(2):
                first = low if h == 0 else pltpu.roll(low, 64, 1)
                second = top if h == 1 else pltpu.roll(top, 64, 1)
                both = jnp.where(edge_lane < 64, first, jnp.where(edge_lane < 80, second, 0.0))
                edges[src, COLS * k + 32 * h:COLS * k + 32 * h + 32, :] = both.astype(BF)
        halo = edges[src]
        for l in range(LAYERS + 1):
            if l < LAYERS:
                here = chunk[src, EDGE + l * PART:EDGE + (l + 1) * PART, :]
            else:
                here = above[src, EDGE:EDGE + PART, :]
            got = jnp.dot(jnp.concatenate([here, halo], axis=1), w_ref[l], preferred_element_type=F32)
            fbuf[l] = got.reshape(3, COLS, 4 * TILE)

        @pl.loop(0, COLS // 16)
        def _(r):
            rows = pl.ds(pl.multiple_of(r * 16, 16), 16)
            dest = pl.ds(pl.multiple_of(src * COLS + r * 16, 16), 16)
            carry = [[None] * 3 for _ in range(4)]
            edge = [jnp.zeros((16, TILE), F32) for _ in range(3)]
            for n in range(LAYERS + 1):
                unit = [[None] * 3 for _ in range(4)]
                if n < LAYERS:
                    g = [gbuf[k, n] for k in range(6)]
                    for q in range(4):
                        low, high = [], []
                        for k in range(3):
                            first = fbuf[n, k, rows, q * TILE:(q + 1) * TILE]
                            second = fbuf[n + 1, k, rows, q * TILE:(q + 1) * TILE]
                            both = first + second
                            low.append(first + both)
                            high.append(second + both)

                        def apply(v):
                            return [
                                g[0] * v[0] + g[3] * v[1] + g[4] * v[2],
                                g[3] * v[0] + g[1] * v[1] + g[5] * v[2],
                                g[4] * v[0] + g[5] * v[1] + g[2] * v[2],
                            ]

                        low, high = apply(low), apply(high)
                        for k in range(3):
                            unit[q][k] = low[k] if n == 0 else carry[q][k] + low[k]
                            carry[q][k] = high[k]
                else:
                    unit = carry
                for k in range(3):
                    near = unit[0][k] + jnp.where(not_first, pltpu.roll(unit[1][k], 1, 1), 0.0)
                    far = unit[2][k] + jnp.where(not_first, pltpu.roll(unit[3][k], 1, 1), 0.0)
                    moved = pltpu.roll(far, GY, 1)
                    img[k, dest, n * TILE:(n + 1) * TILE] = (near + jnp.where(inside, moved, 0.0)).astype(BF)
                    if n > 0:
                        moved = pltpu.roll(far, GY * (n + 1), 1)
                    edge[k] = jnp.where((lane >= GY * n) & (lane < GY * (n + 1)), moved, edge[k])
            for k in range(3):
                img[k, dest, KW - TILE:KW] = edge[k].astype(BF)

    wait_all(chunk.at[pl.ds(0, 7), pl.ds(0, EDGE + PART), :], sa)
    groups = ((0, 1, 2), (3,), (4,), (5,), (6,))

    def send_group(g):
        for i in groups[g]:
            for l in range(1, LAYERS):
                send(i, l, sb.at[g], rb)

    def group_left(g):
        wait_all(chunk.at[pl.ds(0, len(groups[g])), pl.ds(EDGE + PART, 3 * PART), :], sb.at[g])

    send_group(0)
    send_group(1)
    send_group(2)
    for j in range(1, 4):
        arrive(j)
    block(0)
    group_left(0)
    send_group(3)
    small0.wait_recv()
    esrc[1] = esrc[0] + e0[...]
    for i in range(7):
        small1(i).start()
    e1[d] = esrc[1]
    for j in range(4, 8):
        arrive(j)
    for j in range(1, 8):
        if j == 3:
            group_left(1)
            send_group(4)
        block(j)
        if j == 4:
            wait_all(e1.at[pl.ds(0, 7)], er.at[1])
            total = e1[0]
            for who in range(1, 8):
                total = total + e1[who]
            esrc[2] = total
            for i in range(7):
                small2(i).start()
            e2[c] = total

    def panel(half):
        total = None
        for k in range(3):
            rhs = []
            for e in range(8):
                rows = pl.ds(pl.multiple_of(EDGE + k * COLS + half * 32, 32), 32)
                tiles = [
                    chunk[e, pl.ds(pl.multiple_of(EDGE + l * PART + k * COLS + half * 32, 32), 32), :]
                    for l in range(LAYERS)]
                tiles.append(above[e, rows, :])
                tiles.append(edges[e, pl.ds(pl.multiple_of(k * COLS + half * 32, 32), 32), :])
                rhs.append(jnp.concatenate(tiles, axis=1))
            got = lax.dot_general(img[k], jnp.concatenate(rhs, axis=0), NT, preferred_element_type=F32)
            total = got if total is None else total + got
        hacc[half] = total

    other = 1 - core
    panel(other)
    def swap(i):
        rows = pl.ds(pl.multiple_of(col_peer(*FAR[i]) * COLS, COLS), COLS)
        return pltpu.make_async_remote_copy(
            src_ref=hacc.at[other, rows, :], dst_ref=hrecv.at[rows, :], send_sem=p0_sem.at[i], recv_sem=p1_sem.at[i],
            device_id=(partner, c), device_id_type=MESH)

    for i in range(8):
        swap(i).start()
    panel(core)

    wait_all(e2.at[pl.ds(0, 7)], er.at[2])

    me = c * 8 + d
    group = lane // 32
    for i in range(8):
        to_c = col_peer(*FAR[i])
        swap(i).wait_recv()
        sums = []
        for g in range(4):
            rows = pl.ds(pl.multiple_of(to_c * COLS + 16 * g, 16), 16)
            sums.append(hacc[core, rows, :] + hrecv[rows, :])
        for e in range(8):
            a, b = e // 4, e % 4
            packed = None
            for g in range(4):
                piece = sums[g][:, a * TILE:(a + 1) * TILE]
                shift = (32 * g - 32 * b) % TILE
                if shift:
                    piece = pltpu.roll(piece, shift, 1)
                packed = piece if packed is None else jnp.where(group == g, piece, packed)
            pack[to_c * 8 + e] = packed
        for j in range(8):
            if i + j == 14:
                continue
            to_d = slab_peer(*FAR[j]) // 2
            pltpu.make_async_remote_copy(
                src_ref=pack.at[to_c * 8 + to_d], dst_ref=parts.at[me], send_sem=msem, recv_sem=rsem,
                device_id=(to_d * 2 + core, to_c), device_id_type=MESH).start()
    parts[me] = pack[me]

    zone = e2[0]
    for who in range(1, 8):
        zone = zone + e2[who]
    out_ref[36:40, :] = zone[4:8] * (WIDTH / 65536)
    left = iota((1, TILE), 1) < COLS
    for t in range(4):
        out_ref[32 + t:33 + t, :] = jnp.where(left, e2[2 * t, 0:1, :], pltpu.roll(e2[2 * t + 1, 0:1, :], COLS, 1))

    wait_all(parts.at[pl.ds(0, 63)], rsem)
    total = parts[0]
    for who in range(1, 64):
        total = total + parts[who]
    rows = [pltpu.roll(total, TILE - 32 * g, 1) if g else total for g in range(4)]
    out_ref[0:32, 0:COLS] = jnp.transpose(jnp.concatenate(rows, axis=0))[0:32, :]

    @pl.when(s > 0)
    def _():
        for j in range(8):
            forward(j).wait_send()

    group_left(2)
    group_left(3)
    group_left(4)
    small0.wait_send()
    wait_all(e1.at[pl.ds(0, 7)], es.at[1])
    wait_all(e2.at[pl.ds(0, 7)], es.at[2])
    for i in range(8):
        swap(i).wait_send()
    wait_all(parts.at[pl.ds(0, 63)], msem)


def on_device(sensitivity, residual_force, moments, zone_label, misfit):
    any_spec = pl.BlockSpec(memory_space=pl.ANY)
    vmem = pl.BlockSpec(memory_space=pltpu.VMEM)
    dma = pltpu.SemaphoreType.DMA
    out = pl.pallas_call(
        kernel,
        name="gauss_newton",
        out_shape=jax.ShapeDtypeStruct((40, TILE), F32),
        in_specs=[any_spec] * 5,
        out_specs=vmem,
        scratch_shapes=[
            pltpu.VMEM((LAYERS + 1, 2 * TILE, 4 * TILE), BF),
            pltpu.VMEM((2 * LAYERS * TILE, TILE), BF),
            pltpu.VMEM((3, LAYERS * PLANE), BF),
            pltpu.VMEM((6, LAYERS, PLANE), F32),
            pltpu.VMEM((LAYERS, PLANE), jnp.int32),
            pltpu.VMEM((LAYERS, PLANE), F32),
            pltpu.VMEM((3, COLS, LAYERS * PLANE), BF),
            pltpu.VMEM((8, EDGE, TILE), BF),
            pltpu.VMEM((8, CHUNK, TILE), BF),
            pltpu.VMEM((8, EDGE + PART, TILE), BF),
            pltpu.VMEM((8, PART, TILE), BF),
            pltpu.VMEM((3, WIDTH, KW), BF),
            pltpu.VMEM((LAYERS + 1, 3, COLS, 4 * TILE), F32),
            pltpu.VMEM((6, LAYERS, 16, TILE), F32),
            pltpu.VMEM((2, WIDTH, 256), F32),
            pltpu.VMEM((WIDTH, 256), F32),
            pltpu.VMEM((64, 16, TILE), F32),
            pltpu.VMEM((64, 16, TILE), F32),
            pltpu.VMEM((3, 8, TILE), F32),
            pltpu.VMEM((8, TILE), F32),
            pltpu.VMEM((8, 8, TILE), F32),
            pltpu.VMEM((8, 8, TILE), F32),
            dma((4,)), dma((2,)), dma(()), dma((5,)), dma((8,)), dma((8,)), dma((8,)), dma((8,)), dma((8,)), dma((8,)),
            dma((3,)), dma((3,)), dma(()), dma(()),
        ],
        compiler_params=pltpu.CompilerParams(collective_id=0, has_side_effects=True, vmem_limit_bytes=67043328),
    )(sensitivity, residual_force, moments, zone_label, misfit)
    return out[0:32, 0:COLS].T, out[32:36].reshape(WIDTH), out[36:40].reshape(WIDTH)


def solution(mesh):
    in_specs = (
        P(None, "col", "slab"),
        P(None, "slab"),
        P(None, "slab", None),
        P("slab", None),
        P("slab", None),
    )
    out_specs = (P("col", "slab"), P(), P())
    return jax.shard_map(
        on_device, mesh=mesh, in_specs=in_specs, out_specs=out_specs, check_vma=False
    )
```
